32 devices in a mesh: dp: 8 (over z, x), tensor: 4 (over y, core).
Axes of the slice: x: 2, y: 2, z: 4, core: 2. Of those that a mesh axis runs over, the one named last changes fastest.
Arguments:
- tokens: bfloat16 [16384, 480], P(('dp', 'tensor')), may hold values from -6 to 6
- cotangent: bfloat16 [16384, 480], P(('dp', 'tensor')), may hold values from -6 to 6
- lengths: int32 [32], P('dp'), may hold values from 64 to 512, as said below
- clusters: int32 [32], P('dp'), may hold values from 0 to 63
- cluster_weight: float32 [64], replicated, may hold values from 0.5 to 2
- qkv_master: float32 [4, 172800], P('tensor', 'dp'), may hold values from -0.25 to 0.25
- qkv_moment: float32 [4, 172800], P('tensor', 'dp'), may hold values from -160 to 160
- qkv_square: float32 [4, 172800], P('tensor', 'dp'), may hold values from 737.28 to 2949.12
- qkv_ema: float32 [4, 172800], P('tensor', 'dp'), may hold values from -0.25 to 0.25
- out_master: float32 [4, 57600], P('tensor', 'dp'), may hold values from -1.5 to 1.5
- out_moment: float32 [4, 57600], P('tensor', 'dp'), may hold values from -56 to 56
- out_square: float32 [4, 57600], P('tensor', 'dp'), may hold values from 81.92 to 327.68
- out_ema: float32 [4, 57600], P('tensor', 'dp'), may hold values from -1.5 to 1.5
- up_master: float32 [921600], P(('dp', 'tensor')), may hold values from -0.25 to 0.25
- up_moment: float32 [921600], P(('dp', 'tensor')), may hold values from -160 to 160
- up_square: float32 [921600], P(('dp', 'tensor')), may hold values from 737.28 to 2949.12
- up_ema: float32 [921600], P(('dp', 'tensor')), may hold values from -0.25 to 0.25
- down_master: float32 [921600], P(('dp', 'tensor')), may hold values from -0.125 to 0.125
- down_moment: float32 [921600], P(('dp', 'tensor')), may hold values from -320 to 320
- down_square: float32 [921600], P(('dp', 'tensor')), may hold values from 2949.12 to 11796.48
- down_ema: float32 [921600], P(('dp', 'tensor')), may hold values from -0.125 to 0.125
- norm_master: float32 [4, 480], replicated
- norm_moment: float32 [4, 480], replicated, may hold values from -512 to 512
- norm_square: float32 [4, 480], replicated, may hold values from 8192 to 32768
- norm_ema: float32 [4, 480], replicated
Outputs:
- layer_out: float32 [16384, 480], P(('dp', 'tensor'))
- tokens_grad: float32 [16384, 480], P(('dp', 'tensor'))
- qkv_new: float32 [4, 172800], P('tensor', 'dp')
- qkv_moment_new: float32 [4, 172800], P('tensor', 'dp')
- qkv_square_new: float32 [4, 172800], P('tensor', 'dp')
- qkv_ema_new: float32 [4, 172800], P('tensor', 'dp')
- out_new: float32 [4, 57600], P('tensor', 'dp')
- out_moment_new: float32 [4, 57600], P('tensor', 'dp')
- out_square_new: float32 [4, 57600], P('tensor', 'dp')
- out_ema_new: float32 [4, 57600], P('tensor', 'dp')
- up_new: float32 [921600], P(('dp', 'tensor'))
- up_moment_new: float32 [921600], P(('dp', 'tensor'))
- up_square_new: float32 [921600], P(('dp', 'tensor'))
- up_ema_new: float32 [921600], P(('dp', 'tensor'))
- down_new: float32 [921600], P(('dp', 'tensor'))
- down_moment_new: float32 [921600], P(('dp', 'tensor'))
- down_square_new: float32 [921600], P(('dp', 'tensor'))
- down_ema_new: float32 [921600], P(('dp', 'tensor'))
- norm_new: float32 [4, 480], replicated
- norm_moment_new: float32 [4, 480], replicated
- norm_square_new: float32 [4, 480], replicated
- norm_ema_new: float32 [4, 480], replicated
The draws below stay inside these ranges and needn't reach their ends.
Inputs may be any that keep to these rules, and one draw needn't show every extreme that they name: `lengths`: protein 0 has length 512; token slots at positions >= a protein's length are padding.
All inputs are finite; a program needn't handle non-finite values.
Results may differ from the reference program's by a relative error of at most 0.009.
The reference program's roundings to bfloat16 on the way count: a program that leaves them out, or rounds other values in their place, can miss the bound.
Values may be sent and summed in bfloat16 or wider, within the bound.
A program may use at most 256 MiB of HBM per device.

```python
import math
import jax
import jax.numpy as jnp
from jax import lax

D = 480
HEAD = 24
FF = 1920
HEADS_DEV = 5
HEADS = 20
MAXLEN = 512
NCLUST = 64
NPROT = 32
TOKENS = 16384
N_TENSOR = 4


def draw_lengths(key, part):
    pieces = jax.random.split(key, 4)
    summed = jnp.zeros((NPROT,), jnp.int32)
    for number in range(4):
        summed = summed + jax.random.randint(pieces[number], (NPROT,), 0, MAXLEN // 4 + 1)
    summed = jnp.maximum(summed, MAXLEN // 8)
    return summed.at[0].set(MAXLEN)


def norm_rows_draw(key):
    noise = jax.random.normal(key, (4, D), jnp.float32)
    parity = (jnp.arange(4, dtype=jnp.int32) % 2 == 0)[:, None]
    return jnp.where(parity, 1.0 + 0.2 * noise, 0.3 * noise)


def draw_norm_master(key, part):
    return norm_rows_draw(jax.random.fold_in(key, 11))


def draw_norm_ema(key, part):
    return norm_rows_draw(jax.random.fold_in(key, 23))


def touch_ends(drawn, key, smallest, top_value):
    longest = drawn.shape.index(max(drawn.shape))
    spots = []
    for shift in (0, 1):
        where = [jax.random.randint(jax.random.fold_in(key, axis), (), 0, length) for axis, length in enumerate(drawn.shape)]
        where[longest] = (where[longest] + shift) % drawn.shape[longest]
        spots.append(tuple(where))
    return drawn.at[spots[0]].set(smallest).at[spots[1]].set(top_value)


def levels(key, extent, cuts, least, high):
    loudness, own = 1.0, jax.random.fold_in(key, 6)
    for dim, parts in cuts:
        heights = jnp.exp(jax.random.uniform(jax.random.fold_in(own, dim), (parts,), jnp.float32, least / len(cuts), high / len(cuts)))
        loudness = loudness * jnp.repeat(heights, extent[dim] // parts).reshape([-1 if axis == dim else 1 for axis in range(len(extent))])
    return loudness


def gaussian(rng, dims, scale, most, cuts=(), kind=jnp.bfloat16):
    level = levels(rng, dims, cuts, -0.22, 0.18) if cuts else 1.0
    drawn = jax.random.normal(rng, dims, jnp.float32) * scale * level
    return jnp.minimum(jnp.maximum(drawn, -most), most).astype(kind)


def setup_inputs(seed: int = 0) -> dict:
    splits = jax.random.split(jax.random.key(seed), 26)
    tokens = gaussian(splits[0], (TOKENS, D), 1.0, 6.0, ((0, 32),))
    cotangent = gaussian(splits[1], (TOKENS, D), 1.0, 6.0, ((0, 32),))
    lengths = draw_lengths(jax.random.fold_in(splits[25], 71), 0)
    clusters = touch_ends(jax.random.randint(splits[3], (NPROT,), 0, NCLUST), jax.random.fold_in(splits[3], 1), 0, NCLUST - 1).astype(jnp.int32)
    cluster_weight = jnp.clip(jnp.exp(jax.random.uniform(splits[4], (NCLUST,), jnp.float32, math.log(0.5), math.log(2.0))), 0.5, 2.0)
    qkv_master = gaussian(splits[5], (N_TENSOR, D * 3 * HEADS_DEV * HEAD), D ** -0.5, 0.25, ((0, 4), (1, 8)), jnp.float32)
    qkv_moment = gaussian(splits[6], (N_TENSOR, D * 3 * HEADS_DEV * HEAD), (0.3 * (TOKENS // 2) ** 0.5), 160.0, ((0, 4), (1, 8)), jnp.float32)
    qkv_square = jnp.clip(jnp.exp(math.log(2949.12) - 1.3862944 * jax.random.uniform(splits[7], (N_TENSOR, D * 3 * HEADS_DEV * HEAD), jnp.float32) ** levels(splits[7], (N_TENSOR, D * 3 * HEADS_DEV * HEAD), ((0, 4), (1, 8)), -0.2, 0.2)), 737.28, 2949.12)
    qkv_ema = gaussian(splits[8], (N_TENSOR, D * 3 * HEADS_DEV * HEAD), D ** -0.5, 0.25, ((0, 4), (1, 8)), jnp.float32)
    out_master = gaussian(splits[9], (N_TENSOR, HEADS_DEV * HEAD * D), (D // 32) ** -0.5, 1.5, ((0, 4), (1, 8)), jnp.float32)
    out_moment = gaussian(splits[10], (N_TENSOR, HEADS_DEV * HEAD * D), (0.1 * (TOKENS // 2) ** 0.5), 56.0, ((0, 4), (1, 8)), jnp.float32)
    out_square = jnp.clip(jnp.exp(math.log(327.68) - 1.3862944 * jax.random.uniform(splits[11], (N_TENSOR, HEADS_DEV * HEAD * D), jnp.float32) ** levels(splits[11], (N_TENSOR, HEADS_DEV * HEAD * D), ((0, 4), (1, 8)), -0.2, 0.2)), 81.92, 327.68)
    out_ema = gaussian(splits[12], (N_TENSOR, HEADS_DEV * HEAD * D), (D // 32) ** -0.5, 1.5, ((0, 4), (1, 8)), jnp.float32)
    up_master = gaussian(splits[13], (D * FF,), D ** -0.5, 0.25, ((0, 32),), jnp.float32)
    up_moment = gaussian(splits[14], (D * FF,), (0.3 * (TOKENS // 2) ** 0.5), 160.0, ((0, 32),), jnp.float32)
    up_square = jnp.clip(jnp.exp(math.log(2949.12) - 1.3862944 * jax.random.uniform(splits[15], (D * FF,), jnp.float32) ** levels(splits[15], (D * FF,), ((0, 32),), -0.2, 0.2)), 737.28, 2949.12)
    up_ema = gaussian(splits[16], (D * FF,), D ** -0.5, 0.25, ((0, 32),), jnp.float32)
    down_master = gaussian(splits[17], (FF * D,), FF ** -0.5, 0.125, ((0, 32),), jnp.float32)
    down_moment = gaussian(splits[18], (FF * D,), (0.6 * (TOKENS // 2) ** 0.5), 320.0, ((0, 32),), jnp.float32)
    down_square = jnp.clip(jnp.exp(math.log(11796.48) - 1.3862944 * jax.random.uniform(splits[19], (FF * D,), jnp.float32) ** levels(splits[19], (FF * D,), ((0, 32),), -0.2, 0.2)), 2949.12, 11796.48)
    down_ema = gaussian(splits[20], (FF * D,), FF ** -0.5, 0.125, ((0, 32),), jnp.float32)
    norm_master = draw_norm_master(jax.random.fold_in(splits[25], 71), 0)
    norm_moment = gaussian(splits[22], (4, D), ((TOKENS // 2) ** 0.5), 512.0, (), jnp.float32)
    norm_square = jnp.clip(jnp.exp(jax.random.uniform(splits[23], (4, D), jnp.float32, math.log(8192.0), math.log(32768.0))), 8192.0, 32768.0)
    norm_ema = draw_norm_ema(jax.random.fold_in(splits[25], 71), 0)
    return {"tokens": tokens, "cotangent": cotangent, "lengths": lengths, "clusters": clusters, "cluster_weight": cluster_weight, "qkv_master": qkv_master, "qkv_moment": qkv_moment, "qkv_square": qkv_square, "qkv_ema": qkv_ema, "out_master": out_master, "out_moment": out_moment, "out_square": out_square, "out_ema": out_ema, "up_master": up_master, "up_moment": up_moment, "up_square": up_square, "up_ema": up_ema, "down_master": down_master, "down_moment": down_moment, "down_square": down_square, "down_ema": down_ema, "norm_master": norm_master, "norm_moment": norm_moment, "norm_square": norm_square, "norm_ema": norm_ema}


@jax.custom_vjp
def low(v):
    return lax.optimization_barrier(v.astype(jnp.bfloat16)).astype(jnp.float32)

@jax.custom_vjp
def low_back(v):
    return v

def low_keep(v):
    return (low(v), None)

def low_pass(kept, grad):
    return (grad,)

def back_keep(v):
    return (v, None)

def back_low(kept, grad):
    return (low(grad),)
low.defvjp(low_keep, low_pass)
low_back.defvjp(back_keep, back_low)
norm_eps = 1e-05
beta_one = 0.5
beta_two = 0.5
adam_eps = 1e-08
decay_rate = 0.01
average_keep = 0.75
rope_base = 10000.0
masked_score = -1e+30
top_precision = lax.Precision.HIGHEST

def layer_norm(values, gain, shift):
    middle = lax.optimization_barrier(jnp.mean(values, axis=-1, keepdims=True))
    centered = values - middle
    spread = lax.optimization_barrier(jnp.mean(centered * centered, axis=-1, keepdims=True))
    return centered * lax.rsqrt(spread + norm_eps) * gain + shift

def rope_tables(count):
    position = (jnp.arange(count, dtype=jnp.int32) % MAXLEN).astype(jnp.float32)
    exponent = jnp.arange(HEAD // 2, dtype=jnp.float32) * (2.0 / HEAD)
    inverse_freq = rope_base ** (-exponent)
    angle = position[:, None] * inverse_freq[None, :]
    cosine = jnp.cos(angle)
    sine_table = jnp.sin(angle)
    return (jnp.concatenate([cosine, cosine], -1), jnp.concatenate([sine_table, sine_table], -1))

def rotate(block, cosine, sine_table):
    half_size = HEAD // 2
    turned = jnp.concatenate([-block[..., half_size:], block[..., :half_size]], -1)
    return block * cosine[:, None, :] + turned * sine_table[:, None, :]

def attend_one(inputs):
    queries, key_rows, vectors, length = inputs
    scores = jnp.einsum('qhe,khe->hqk', queries, key_rows, precision=top_precision) * HEAD ** (-0.5)
    usable = jnp.arange(MAXLEN, dtype=jnp.int32) < length
    scores = low_back(jnp.where(usable[None, None, :], scores, masked_score))
    probability = low(jax.nn.softmax(scores, axis=-1))
    return jnp.einsum('hqk,khe->qhe', probability, vectors, precision=top_precision)

def adam_step(master, moment, square, average, grad, rate):
    moment_new = beta_one * moment + (1.0 - beta_one) * grad
    square_new = beta_two * square + (1.0 - beta_two) * grad * grad
    update = moment_new / (jnp.sqrt(square_new) + adam_eps) + decay_rate * master
    fresh = master - rate * update
    average_new = average_keep * average + (1.0 - average_keep) * fresh
    return (fresh, moment_new, square_new, average_new)

def reference(tokens, cotangent, lengths, clusters, cluster_weight, qkv_master, qkv_moment, qkv_square, qkv_ema, out_master, out_moment, out_square, out_ema, up_master, up_moment, up_square, up_ema, down_master, down_moment, down_square, down_ema, norm_master, norm_moment, norm_square, norm_ema):
    head_width = HEADS_DEV * HEAD

    def forward(inputs, norms, joined_weight, out_weight, up_weight, down_weight):
        normed = low(layer_norm(inputs, norms[0], norms[1]))
        joined_rows = low_back(jnp.einsum('nd,tdc->ntc', normed, low(joined_weight), precision=top_precision))
        cosine, sine_table = rope_tables(TOKENS)
        queries = low(rotate(joined_rows[:, :, :head_width].reshape(TOKENS, HEADS, HEAD), cosine, sine_table))
        key_rows = low(rotate(joined_rows[:, :, head_width:2 * head_width].reshape(TOKENS, HEADS, HEAD), cosine, sine_table))
        vectors = low(joined_rows[:, :, 2 * head_width:].reshape(TOKENS, HEADS, HEAD))
        block_shape = (NPROT, MAXLEN, HEADS, HEAD)
        attended = lax.map(jax.checkpoint(attend_one), (queries.reshape(block_shape), key_rows.reshape(block_shape), vectors.reshape(block_shape), lengths))
        attended = low(low_back(attended.reshape(TOKENS, HEADS * HEAD)))
        residual = inputs + low_back(jnp.dot(attended, low(out_weight), precision=top_precision))
        normed_two = low(layer_norm(residual, norms[2], norms[3]))
        upper_pre = low_back(jnp.dot(normed_two, low(up_weight), precision=top_precision))
        active = low(jax.nn.gelu(upper_pre, approximate=False))
        return residual + low_back(jnp.dot(active, low(down_weight), precision=top_precision))
    tok_float = tokens.astype(jnp.float32)
    joined_weight = qkv_master.reshape(N_TENSOR, D, 3 * head_width)
    out_weight = out_master.reshape(HEADS * HEAD, D)
    up_weight = up_master.reshape(D, FF)
    down_weight = down_master.reshape(FF, D)
    layer_out, pullback = jax.vjp(forward, tok_float, norm_master, joined_weight, out_weight, up_weight, down_weight)
    slot = jnp.arange(TOKENS, dtype=jnp.int32)
    protein = slot // MAXLEN
    per_protein = cluster_weight[clusters]
    row_scale = jnp.where(slot % MAXLEN < lengths[protein], per_protein[protein], 0.0)
    grads = pullback(cotangent.astype(jnp.float32) * row_scale[:, None])
    tokens_grad, norm_grad, joined_grad, out_grad, up_grad, down_grad = grads
    qkv_all = adam_step(qkv_master, qkv_moment, qkv_square, qkv_ema, joined_grad.reshape(N_TENSOR, -1), D ** (-0.5))
    out_all = adam_step(out_master, out_moment, out_square, out_ema, out_grad.reshape(N_TENSOR, -1), (D // 32) ** (-0.5))
    up_all = adam_step(up_master, up_moment, up_square, up_ema, up_grad.reshape(-1), D ** (-0.5))
    down_all = adam_step(down_master, down_moment, down_square, down_ema, down_grad.reshape(-1), FF ** (-0.5))
    norm_all = adam_step(norm_master, norm_moment, norm_square, norm_ema, norm_grad, 0.2)
    return (layer_out, tokens_grad, qkv_all[0], qkv_all[1], qkv_all[2], qkv_all[3], out_all[0], out_all[1], out_all[2], out_all[3], up_all[0], up_all[1], up_all[2], up_all[3], down_all[0], down_all[1], down_all[2], down_all[3], norm_all[0], norm_all[1], norm_all[2], norm_all[3])
```

```python
import jax
import jax.numpy as jnp
import numpy as np
from jax import lax
from jax.experimental import pallas as pl
from jax.experimental.pallas import tpu as pltpu
from jax.sharding import PartitionSpec as P

D = 480
HEAD = 24
FF = 1920
MAXLEN = 512
NDP, NTEN = 8, 4
WIDE = 512
HEADS_DEV = 5
LANES = 128
TILES = 47
UP0, DOWN0, QKV0, OUT0 = 0, 15, 31, 43
CHUNK = 384
QB = 256

norm_eps = 1e-05
beta_one = 0.5
beta_two = 0.5
adam_eps = 1e-08
decay_rate = 0.01
average_keep = 0.75
masked_score = -1e30
MESH = pl.DeviceIdType.MESH
f32, bf16 = jnp.float32, jnp.bfloat16


def mm(a, b):
    return lax.dot_general(a, b, (((1,), (0,)), ((), ())), preferred_element_type=f32)


def mm_nt(a, b):
    return lax.dot_general(a, b, (((1,), (1,)), ((), ())), preferred_element_type=f32)


def constants():
    natural = np.arange(D)
    squeeze = np.zeros((WIDE, WIDE), np.float32)
    squeeze[natural, 16 * (natural // 15) + natural % 15] = 1.0
    spread = np.zeros((CHUNK, CHUNK), np.float32)
    for third in range(3):
        lane = np.arange(120)
        spread[third * 120 + lane, third * 128 + lane] = 1.0
    position = np.arange(MAXLEN, dtype=np.float32)
    exponent = np.arange(HEAD // 2, dtype=np.float32) * np.float32(2.0 / HEAD)
    inverse = np.float32(10000.0) ** (-exponent)
    angle = (position[:, None] * inverse[None, :]).astype(np.float32).astype(np.float64)
    lane = np.arange(120)
    place = lane % HEAD
    cosine = np.zeros((MAXLEN, LANES), np.float32)
    first = np.zeros((MAXLEN, LANES), np.float32)
    second = np.zeros((MAXLEN, LANES), np.float32)
    cosine[:, :120] = np.cos(angle)[:, place % 12]
    sines = np.sin(angle)[:, place % 12]
    first[:, :120] = np.where(place < 12, -sines, 0.0)
    second[:, :120] = np.where(place >= 12, sines, 0.0)
    low = lambda v: jnp.asarray(v.astype(jnp.bfloat16))
    return (low(squeeze), low(squeeze.T), low(spread), jnp.asarray(cosine), jnp.asarray(first), jnp.asarray(second))


def gelu_parts(u):
    half = 0.5 * (1.0 + lax.erf(u * 0.7071067811865476))
    return u * half, half + u * jnp.exp(-0.5 * u * u) * 0.3989422804014327


def layer_kernel(
    lengths, clusters, weights_of, W, tok, cot, norm, squeeze, widen, spread, cosine, first, second,
    layer_out, tokens_grad, G, norm_grad,
    up_s, down_s, qkv_s, out_s, q_s, k_s, v_s, kT_s, vT_s, P_s, OT_s, att_s, dA_s, dqT_s, dk_s, dv_s,
    act1_s, act2_s, act_pad, plain1, plain2, res_s, y_s, dn_s, dres_s, dlow_s, active_s, gdown_s, x_s,
):
    me = lax.axis_index("tensor")
    length = lengths[me]
    scale_row = weights_of[clusters[me]]
    scale = HEAD ** -0.5

    sq = squeeze[...]

    def up_tile(c, carry):
        part = mm(sq, W[:, :, UP0 + c].reshape(WIDE, LANES)).astype(bf16)
        up_s[:, pl.ds(pl.multiple_of(c * LANES, LANES), LANES)] = part
        return carry

    for c in range(15):
        up_tile(c, 0)
    for t in range(NTEN):
        pieces = [W[:, t, QKV0 + 4 * c : QKV0 + 4 * c + 4].reshape(WIDE, LANES) for c in range(3)]
        plain = mm(sq, jnp.concatenate(pieces, 1)).astype(bf16)
        qkv_s[t] = mm(plain, spread[...]).astype(bf16)
        pieces = [W[:, t, OUT0 + c].reshape(LANES, LANES) for c in range(4)]
        out_s[t] = mm(squeeze[:LANES, :LANES], jnp.concatenate(pieces, 1)).astype(bf16)

    def down_rows(k, carry):
        pieces = [W[k, :, DOWN0 + 4 * c : DOWN0 + 4 * c + 4].reshape(256, LANES) for c in range(4)]
        part = mm(squeeze[:240, :256], jnp.concatenate(pieces, 1)).astype(bf16)
        down_s[pl.ds(pl.multiple_of(k * 240, 16), 240), :] = part
        return carry

    lax.fori_loop(0, 8, down_rows, 0)

    lane = lax.broadcasted_iota(jnp.int32, (1, WIDE), 1)
    real = jnp.where(lane < D, 1.0, 0.0)
    gains = norm[...]

    def norm_rows(values, gain, shift):
        middle = jnp.sum(values, axis=-1, keepdims=True) * (1.0 / D)
        centered = (values - middle) * real
        spread_ = jnp.sum(centered * centered, axis=-1, keepdims=True) * (1.0 / D)
        inverse = lax.rsqrt(spread_ + norm_eps)
        plain = centered * inverse
        return plain * gain + shift, plain, inverse

    def norm_back(dz, plain, inverse, gain):
        dg = jnp.sum(dz * plain, axis=0, keepdims=True)
        db = jnp.sum(dz, axis=0, keepdims=True)
        scaled = dz * gain
        one = jnp.sum(scaled, axis=-1, keepdims=True) * (1.0 / D)
        two = jnp.sum(scaled * plain, axis=-1, keepdims=True) * (1.0 / D)
        return inverse * (scaled - one - plain * two) * real, dg, db

    x_s[...] = jnp.zeros_like(x_s)
    x_s[:, :D] = tok[...].astype(f32)
    normed, plain, inverse1 = norm_rows(x_s[...], gains[0:1], gains[1:2])
    plain1[...] = plain
    act1_s[...] = normed.astype(bf16)
    cosv, firstv, secondv = cosine[...], first[...], second[...]
    for t in range(NTEN):
        joined = mm(act1_s[...], qkv_s[t])
        for number in range(2):
            u = joined[:, number * LANES : (number + 1) * LANES]
            r = u * cosv + pltpu.roll(u, LANES - 12, 1) * firstv + pltpu.roll(u, 12, 1) * secondv
            if number == 0:
                q_s[t] = r.astype(bf16)
            else:
                k_s[t] = r.astype(bf16)
                kT_s[t] = r.T.astype(bf16)
        v = joined[:, 2 * LANES :]
        v_s[t] = v.astype(bf16)
        vT_s[t] = v.T.astype(bf16)

    lane_id = lax.broadcasted_iota(jnp.int32, (1, LANES), 1)
    row_id = lax.broadcasted_iota(jnp.int32, (LANES, 1), 0)
    key_id = lax.broadcasted_iota(jnp.int32, (MAXLEN, 1), 0)
    usable = key_id < length

    OT_s[...] = jnp.zeros_like(OT_s)

    def forward_head(h, carry):
        t = h // HEADS_DEV
        begin = (h - t * HEADS_DEV) * HEAD
        lanes = jnp.where((lane_id >= begin) & (lane_id < begin + HEAD), 1.0, 0.0).astype(bf16)
        rows = jnp.where((row_id >= begin) & (row_id < begin + HEAD), 1.0, 0.0).astype(bf16)
        keys = k_s[t] * lanes
        values = vT_s[t] * rows
        for b in range(MAXLEN // QB):
            cols = slice(b * QB, (b + 1) * QB)
            s = mm_nt(keys, q_s[t, cols, :])
            s = jnp.where(usable, s * scale, masked_score)
            top = jnp.max(s, axis=0, keepdims=True)
            e = jnp.exp(s - top)
            total = jnp.sum(e, axis=0, keepdims=True)
            p = (e * (1.0 / total)).astype(bf16)
            P_s[h, :, cols] = p
            OT_s[t, :, cols] += mm(values, p)
        return carry

    lax.fori_loop(0, NTEN * HEADS_DEV, forward_head, 0)

    res = x_s[...]
    for t in range(NTEN):
        att_s[t] = OT_s[t].T.astype(bf16)
        res = res + mm(att_s[t], out_s[t])
    res_s[...] = res
    normed, plain, inverse2 = norm_rows(res, gains[2:3], gains[3:4])
    plain2[...] = plain
    act2_s[...] = normed.astype(bf16)
    act_pad[...] = mm_nt(widen[...], act2_s[...]).astype(bf16)

    row = lax.broadcasted_iota(jnp.int32, (MAXLEN, 1), 0)
    row_scale = jnp.where(row < length, scale_row, 0.0)
    grad = cot[...].astype(f32) * row_scale
    dres_s[...] = jnp.zeros_like(dres_s)
    dres_s[:, :D] = grad
    dlow_s[...] = dres_s[...].astype(bf16)

    y_s[...] = res_s[...]
    dn_s[...] = jnp.zeros_like(dn_s)
    eye_row = lax.broadcasted_iota(jnp.int32, (CHUNK, CHUNK), 0)
    eye_col = lax.broadcasted_iota(jnp.int32, (CHUNK, CHUNK), 1)
    eye = jnp.where(eye_row == eye_col, 1.0, 0.0).astype(bf16)
    active_s[...] = eye

    def hidden_chunk(c, carry):
        cols = pl.ds(pl.multiple_of(c * CHUNK, LANES), CHUNK)
        u = mm(act2_s[...], up_s[:, cols])
        value, slope = gelu_parts(u)
        a = value.astype(bf16)
        y_s[...] += mm(a, down_s[cols, :])
        d_active = mm_nt(dlow_s[...], down_s[cols, :])
        d_upper = (d_active * slope).astype(bf16)
        dn_s[...] += mm_nt(d_upper, up_s[:, cols])
        g_up = mm(act_pad[...], d_upper).astype(bf16)
        for part in range(3):
            G[:, :, UP0 + 3 * c + part] = g_up[:, part * LANES : (part + 1) * LANES].reshape(NDP, NTEN, 16, LANES)
        aT = mm_nt(active_s[...], a).astype(bf16)
        gdown_s[cols, :] = mm(aT, dlow_s[...]).astype(bf16)
        return carry

    lax.fori_loop(0, FF // CHUNK, hidden_chunk, 0)
    layer_out[...] = y_s[:, :D]

    def down_groups(k, carry):
        part = mm(widen[:256, :240], gdown_s[pl.ds(pl.multiple_of(k * 240, 16), 240), :]).astype(bf16)
        for c in range(4):
            G[k, :, DOWN0 + 4 * c : DOWN0 + 4 * c + 4] = part[:, c * LANES : (c + 1) * LANES].reshape(NTEN, 4, 16, LANES)
        return carry

    lax.fori_loop(0, 8, down_groups, 0)

    d_from, dg2, db2 = norm_back(dn_s[...], plain2[...], inverse2, gains[2:3])
    d_res = dres_s[...] + d_from
    dres_s[...] = d_res
    dlow_s[...] = d_res.astype(bf16)

    for t in range(NTEN):
        dA_s[t] = mm_nt(dlow_s[...], out_s[t]).astype(bf16)
        attT = mm_nt(widen[:LANES, :LANES], att_s[t]).astype(bf16)
        part = mm(attT, dlow_s[...]).astype(bf16)
        for c in range(4):
            G[:, t, OUT0 + c] = part[:, c * LANES : (c + 1) * LANES].reshape(NDP, 16, LANES)

    dqT_s[...] = jnp.zeros_like(dqT_s)
    dk_s[...] = jnp.zeros_like(dk_s)
    dv_s[...] = jnp.zeros_like(dv_s)

    def backward_head(h, carry):
        t = h // HEADS_DEV
        begin = (h - t * HEADS_DEV) * HEAD
        lanes = jnp.where((lane_id >= begin) & (lane_id < begin + HEAD), 1.0, 0.0).astype(bf16)
        rows = jnp.where((row_id >= begin) & (row_id < begin + HEAD), 1.0, 0.0).astype(bf16)
        values = v_s[t]
        keysT = kT_s[t] * rows
        for b in range(MAXLEN // QB):
            cols = slice(b * QB, (b + 1) * QB)
            dA = dA_s[t, cols, :] * lanes
            dP = mm_nt(values, dA)
            low = P_s[h, :, cols]
            p = low.astype(f32)
            centre = jnp.sum(p * dP, axis=0, keepdims=True)
            ds = (p * (dP - centre)).astype(bf16)
            dv_s[t] += mm(low, dA)
            dk_s[t] += mm(ds, q_s[t, cols, :] * lanes)
            dqT_s[t, :, cols] += mm(keysT, ds)
        return carry

    lax.fori_loop(0, NTEN * HEADS_DEV, backward_head, 0)

    act_pad[...] = mm_nt(widen[...], act1_s[...]).astype(bf16)
    dz = jnp.zeros((MAXLEN, WIDE), f32)
    for t in range(NTEN):
        pieces = []
        for number in range(2):
            g = (dqT_s[t].T if number == 0 else dk_s[t]) * scale
            r = g * cosv - pltpu.roll(g, LANES - 12, 1) * firstv - pltpu.roll(g, 12, 1) * secondv
            pieces.append(r.astype(bf16))
        pieces.append(dv_s[t].astype(bf16))
        d_joined = jnp.concatenate(pieces, 1)
        dz = dz + mm_nt(d_joined, qkv_s[t])
        natural = mm_nt(d_joined, spread[...]).astype(bf16)
        part = mm(act_pad[...], natural).astype(bf16)
        for c in range(3):
            G[:, t, QKV0 + 4 * c : QKV0 + 4 * c + 4] = part[:, c * LANES : (c + 1) * LANES].reshape(NDP, 4, 16, LANES)
    d_from, dg1, db1 = norm_back(dz, plain1[...], inverse1, gains[0:1])
    x_s[...] = dres_s[...] + d_from
    tokens_grad[...] = x_s[:, :D]
    norm_grad[...] = jnp.concatenate([dg1, db1, dg2, db2, jnp.zeros((4, WIDE), f32)], 0)


def run_layer(lengths, clusters, cluster_weight, tiles, tokens, cotangent, norm_master):
    rows = MAXLEN
    wide_norm = jnp.pad(norm_master, ((0, 0), (0, WIDE - D)))
    smem = pl.BlockSpec(memory_space=pltpu.SMEM)
    vmem = pl.BlockSpec(memory_space=pltpu.VMEM)
    head_set = (NTEN, MAXLEN, LANES)
    turned = (NTEN, LANES, MAXLEN)
    wide = (rows, WIDE)
    return pl.pallas_call(
        layer_kernel,
        out_shape=(
            jax.ShapeDtypeStruct((rows, D), f32),
            jax.ShapeDtypeStruct((rows, D), f32),
            jax.ShapeDtypeStruct((NDP, NTEN, TILES, 16, LANES), bf16),
            jax.ShapeDtypeStruct((8, WIDE), f32),
        ),
        in_specs=[smem] * 3 + [vmem] * 10,
        out_specs=[vmem] * 4,
        scratch_shapes=[
            pltpu.VMEM((WIDE, FF), bf16),
            pltpu.VMEM((FF, WIDE), bf16),
            pltpu.VMEM((NTEN, WIDE, CHUNK), bf16),
            pltpu.VMEM((NTEN, LANES, WIDE), bf16),
            pltpu.VMEM(head_set, bf16),
            pltpu.VMEM(head_set, bf16),
            pltpu.VMEM(head_set, bf16),
            pltpu.VMEM(turned, bf16),
            pltpu.VMEM(turned, bf16),
            pltpu.VMEM((NTEN * HEADS_DEV, MAXLEN, MAXLEN), bf16),
            pltpu.VMEM(turned, f32),
            pltpu.VMEM(head_set, bf16),
            pltpu.VMEM(head_set, bf16),
            pltpu.VMEM(turned, f32),
            pltpu.VMEM(head_set, f32),
            pltpu.VMEM(head_set, f32),
            pltpu.VMEM(wide, bf16),
            pltpu.VMEM(wide, bf16),
            pltpu.VMEM(wide, bf16),
            pltpu.VMEM(wide, f32),
            pltpu.VMEM(wide, f32),
            pltpu.VMEM(wide, f32),
            pltpu.VMEM(wide, f32),
            pltpu.VMEM(wide, f32),
            pltpu.VMEM(wide, f32),
            pltpu.VMEM(wide, bf16),
            pltpu.VMEM((CHUNK, CHUNK), bf16),
            pltpu.VMEM((FF, WIDE), bf16),
            pltpu.VMEM(wide, f32),
        ],
        compiler_params=pltpu.CompilerParams(vmem_limit_bytes=60 * 1024 * 1024),
        name="layer",
    )(lengths, clusters, cluster_weight, tiles, tokens, cotangent, wide_norm, *constants())


def shard_tiles(up, down, qkv, out):
    up = jnp.pad(up.reshape(15, 15, LANES), ((0, 1), (0, 0), (0, 0))).transpose(1, 0, 2)
    down = jnp.pad(down.reshape(4, 15, D), ((0, 0), (0, 1), (0, WIDE - D)))
    down = down.reshape(4, 16, 4, LANES).transpose(2, 0, 1, 3).reshape(16, 16, LANES)
    qkv = jnp.pad(qkv.reshape(4, 15, 360), ((0, 0), (0, 1), (0, CHUNK - 360)))
    qkv = qkv.reshape(4, 16, 3, LANES).transpose(2, 0, 1, 3).reshape(12, 16, LANES)
    out = jnp.pad(out.reshape(15, D), ((0, 1), (0, WIDE - D)))
    out = out.reshape(16, 4, LANES).transpose(1, 0, 2)
    return jnp.concatenate([up, down, qkv, out], 0)


def tiles_shard(tiles):
    up = tiles[UP0:DOWN0, :15].transpose(1, 0, 2).reshape(-1)
    down = tiles[DOWN0:QKV0].reshape(4, 4, 16, LANES).transpose(1, 2, 0, 3)[:, :15].reshape(60, WIDE)[:, :D].reshape(-1)
    qkv = tiles[QKV0:OUT0].reshape(3, 4, 16, LANES).transpose(1, 2, 0, 3)[:, :15].reshape(60, CHUNK)[:, :360].reshape(1, -1)
    out = tiles[OUT0:].transpose(1, 0, 2)[:15].reshape(15, WIDE)[:, :D].reshape(1, -1)
    return up, down, qkv, out


ROUTES = (
    (0, 19, (0, 1, 3, 2, 4)),
    (19, 19, (0, 1, 2, 3, 4)),
    (38, 9, (2, 3, 0, 1, 4)),
)


def place():
    dp, tensor = lax.axis_index("dp"), lax.axis_index("tensor")
    return (dp // 4, (dp // 2) % 2, dp % 2, tensor // 2, tensor % 2)


def partner(coords, dim):
    c = list(coords)
    c[dim] = 1 - c[dim]
    return (c[0] * 4 + c[1] * 2 + c[2], c[3] * 2 + c[4])


def greet(coords):
    barrier = pltpu.get_barrier_semaphore()
    for dim in range(5):
        pl.semaphore_signal(barrier, inc=1, device_id=partner(coords, dim), device_id_type=MESH)
    pl.semaphore_wait(barrier, 5)


def gather_kernel(shard, whole, send, recv, own_sem):
    coords = place()
    greet(coords)
    own = pltpu.make_async_copy(shard, whole.at[coords], own_sem)
    own.start()
    copies = [[None] * 5 for _ in ROUTES]
    for stage in range(5):
        for r, (begin, count, order) in enumerate(ROUTES):
            if stage > 0:
                copies[r][stage - 1].wait_recv()
            if stage == 1 and r == 0:
                own.wait()
            done, dim = order[:stage], order[stage]
            where = tuple(slice(None) if d in done else coords[d] for d in range(5)) + (pl.ds(begin, count),)
            copies[r][stage] = pltpu.make_async_remote_copy(
                src_ref=shard.at[pl.ds(begin, count)] if stage == 0 else whole.at[where],
                dst_ref=whole.at[where],
                send_sem=send.at[r, stage],
                recv_sem=recv.at[r, stage],
                device_id=partner(coords, dim),
                device_id_type=MESH,
            )
            copies[r][stage].start()
    for r in range(len(ROUTES)):
        copies[r][4].wait_recv()
    for r in range(len(ROUTES)):
        for stage in range(5):
            copies[r][stage].wait_send()


def gather(shard):
    n = len(ROUTES)
    whole = pl.pallas_call(
        gather_kernel,
        out_shape=jax.ShapeDtypeStruct((2, 2, 2, 2, 2, TILES, 16, LANES), bf16),
        in_specs=[pl.BlockSpec(memory_space=pltpu.VMEM)],
        out_specs=pl.BlockSpec(memory_space=pltpu.VMEM),
        scratch_shapes=[
            pltpu.SemaphoreType.DMA((n, 5)),
            pltpu.SemaphoreType.DMA((n, 5)),
            pltpu.SemaphoreType.DMA,
        ],
        compiler_params=pltpu.CompilerParams(collective_id=0, has_side_effects=True, vmem_limit_bytes=40 << 20),
        name="gather",
    )(shard)
    return whole.reshape(8, 4, TILES, 16, LANES)


def scatter_kernel(parts, norm, total, norm_total, *scratch):
    n = len(ROUTES)
    bufs = [scratch[5 * r : 5 * r + 5] for r in range(n)]
    norm_in, norm_now, send, recv, norm_send, norm_recv = scratch[5 * n :]
    coords = place()
    greet(coords)
    copies = [[None] * 5 for _ in ROUTES]
    norm_copies = [None] * 5

    def source(r, stage, coordinate):
        begin, count, order = ROUTES[r]
        order = order[::-1]
        left = [d for d in range(5) if d not in order[:stage]]
        where = tuple(coordinate if d == order[stage] else slice(None) for d in left)
        if stage == 0:
            return parts, where + (pl.ds(begin, count),)
        return bufs[r][stage - 1], where

    def send_norm(stage):
        c = pltpu.make_async_remote_copy(
            src_ref=norm if stage == 0 else norm_now.at[stage - 1],
            dst_ref=norm_in.at[stage],
            send_sem=norm_send.at[stage],
            recv_sem=norm_recv.at[stage],
            device_id=partner(coords, stage),
            device_id_type=MESH,
        )
        c.start()
        norm_copies[stage] = c

    def send_part(r, stage):
        dim = ROUTES[r][2][::-1][stage]
        ref, where = source(r, stage, 1 - coords[dim])
        c = pltpu.make_async_remote_copy(
            src_ref=ref.at[where],
            dst_ref=bufs[r][stage],
            send_sem=send.at[r, stage],
            recv_sem=recv.at[r, stage],
            device_id=partner(coords, dim),
            device_id_type=MESH,
        )
        c.start()
        copies[r][stage] = c

    send_norm(0)
    for r in range(n):
        send_part(r, 0)
    for stage in range(5):
        for r in range(n):
            begin, count, order = ROUTES[r]
            dim = order[::-1][stage]
            copies[r][stage].wait_recv()
            ref, where = source(r, stage, coords[dim])
            if stage < 4:
                buf = bufs[r][stage]
                buf[...] = buf[...] + ref[where]
                send_part(r, stage + 1)
            else:
                total[begin : begin + count] = bufs[r][stage][...].astype(f32) + ref[where].astype(f32)
        norm_copies[stage].wait_recv()
        now = norm[...] if stage == 0 else norm_now[stage - 1]
        now = now + norm_in[stage]
        if stage < 4:
            norm_now[stage] = now
            send_norm(stage + 1)
        else:
            norm_total[...] = now
    for stage in range(5):
        norm_copies[stage].wait_send()
        for r in range(n):
            copies[r][stage].wait_send()


def scatter(parts, norm):
    n = len(ROUTES)
    vmem = pl.BlockSpec(memory_space=pltpu.VMEM)
    bufs = [
        pltpu.VMEM((2,) * (4 - stage) + (count, 16, LANES), bf16)
        for begin, count, order in ROUTES
        for stage in range(5)
    ]
    return pl.pallas_call(
        scatter_kernel,
        out_shape=(
            jax.ShapeDtypeStruct((TILES, 16, LANES), f32),
            jax.ShapeDtypeStruct((8, WIDE), f32),
        ),
        in_specs=[vmem] * 2,
        out_specs=[vmem] * 2,
        scratch_shapes=bufs
        + [
            pltpu.VMEM((5, 8, WIDE), f32),
            pltpu.VMEM((4, 8, WIDE), f32),
            pltpu.SemaphoreType.DMA((n, 5)),
            pltpu.SemaphoreType.DMA((n, 5)),
            pltpu.SemaphoreType.DMA((5,)),
            pltpu.SemaphoreType.DMA((5,)),
        ],
        compiler_params=pltpu.CompilerParams(collective_id=1, has_side_effects=True, vmem_limit_bytes=40 << 20),
        name="scatter",
    )(parts.reshape(2, 2, 2, 2, 2, TILES, 16, LANES), norm)


def adam_step(master, moment, square, average, grad, rate):
    moment_new = beta_one * moment + (1.0 - beta_one) * grad
    square_new = beta_two * square + (1.0 - beta_two) * grad * grad
    update = moment_new / (jnp.sqrt(square_new) + adam_eps) + decay_rate * master
    fresh = master - rate * update
    average_new = average_keep * average + (1.0 - average_keep) * fresh
    return (fresh, moment_new, square_new, average_new)


def to_groups(up, down, qkv, out):
    up, down = up.reshape(NDP, NTEN, -1), down.reshape(NDP, NTEN, -1)
    qkv = qkv.reshape(NTEN, NDP, -1).transpose(1, 0, 2)
    out = out.reshape(NTEN, NDP, -1).transpose(1, 0, 2)
    return jax.vmap(jax.vmap(shard_tiles))(up, down, qkv, out)


def from_groups(tiles):
    up, down, qkv, out = jax.vmap(jax.vmap(tiles_shard))(tiles.astype(f32))
    qkv = qkv.reshape(NDP, NTEN, -1).transpose(1, 0, 2).reshape(NTEN, -1)
    out = out.reshape(NDP, NTEN, -1).transpose(1, 0, 2).reshape(NTEN, -1)
    return up.reshape(-1), down.reshape(-1), qkv, out


def on_device(tokens, cotangent, lengths, clusters, cluster_weight, *state):
    qkv, out, up, down, norm = (state[4 * k : 4 * k + 4] for k in range(5))
    ends = ("dp", "tensor")
    low = tuple(w[0].astype(bf16) for w in (up, down, qkv, out))
    grid = (lax.axis_size("dp"), lax.axis_size("tensor")) == (NDP, NTEN)
    if grid:
        tiles = gather(shard_tiles(*low))
    else:
        whole = [lax.all_gather(w, ends, axis=0, tiled=True) for w in low[:2]]
        for w in low[2:]:
            block = lax.all_gather(w, "dp", axis=1, tiled=True)
            whole.append(lax.all_gather(block, "tensor", axis=0, tiled=True))
        tiles = to_groups(*whole)
    layer_out, tokens_grad, parts, norm_parts = run_layer(
        lengths, clusters, cluster_weight, tiles, tokens, cotangent, norm[0]
    )
    if grid:
        total, norm_total = scatter(parts, norm_parts)
        grads = tiles_shard(total)
    else:
        whole = from_groups(parts)
        grads = [lax.psum_scatter(g, ends, scatter_dimension=0, tiled=True) for g in whole[:2]]
        for g in whole[2:]:
            block = lax.psum_scatter(g, "tensor", scatter_dimension=0, tiled=True)
            grads.append(lax.psum_scatter(block, "dp", scatter_dimension=1, tiled=True))
        norm_total = lax.psum(norm_parts, ends)
    up_grad, down_grad, qkv_grad, out_grad = grads
    results = (layer_out, tokens_grad)
    results += adam_step(*qkv, qkv_grad, D ** (-0.5))
    results += adam_step(*out, out_grad, (D // 32) ** (-0.5))
    results += adam_step(*up, up_grad, D ** (-0.5))
    results += adam_step(*down, down_grad, FF ** (-0.5))
    results += adam_step(*norm, norm_total[:4, :D], 0.2)
    return results


def solution(mesh):
    rows, both, flat = P(("dp", "tensor"), None), P("tensor", "dp"), P(("dp", "tensor"))
    state = (both,) * 8 + (flat,) * 8 + (P(),) * 4
    return jax.shard_map(
        on_device,
        mesh=mesh,
        in_specs=(rows, rows, P("dp"), P("dp"), P()) + state,
        out_specs=(rows, rows) + state,
        check_vma=False,
    )
```

```python
import functools

import jax
import jax.numpy as jnp
import numpy as np
from jax import lax
from jax.experimental import pallas as pl
from jax.experimental.pallas import tpu as pltpu
from jax.sharding import PartitionSpec as P

D = 480
HEAD = 24
FF = 1920
MAXLEN = 512
NDP, NTEN = 8, 4
WIDE = 512
HEADS_DEV = 5
LANES = 128
TILES = 47
UP0, DOWN0, OUT0, QKV0 = 0, 15, 31, 35
CHUNK = 384
QB = 256

norm_eps = 1e-05
beta_one = 0.5
beta_two = 0.5
adam_eps = 1e-08
decay_rate = 0.01
average_keep = 0.75
masked_score = -1e30
MESH = pl.DeviceIdType.MESH
f32, bf16 = jnp.float32, jnp.bfloat16


def mm(a, b):
    return lax.dot_general(a, b, (((1,), (0,)), ((), ())), preferred_element_type=f32)


def mm_nt(a, b):
    return lax.dot_general(a, b, (((1,), (1,)), ((), ())), preferred_element_type=f32)


def constants():
    natural = np.arange(D)
    squeeze = np.zeros((WIDE, WIDE), np.float32)
    squeeze[natural, 16 * (natural // 15) + natural % 15] = 1.0
    spread = np.zeros((CHUNK, CHUNK), np.float32)
    for third in range(3):
        lane = np.arange(120)
        spread[third * 120 + lane, third * 128 + lane] = 1.0
    position = np.arange(MAXLEN, dtype=np.float32)
    exponent = np.arange(HEAD // 2, dtype=np.float32) * np.float32(2.0 / HEAD)
    inverse = np.float32(10000.0) ** (-exponent)
    angle = (position[:, None] * inverse[None, :]).astype(np.float32).astype(np.float64)
    lane = np.arange(120)
    place = lane % HEAD
    cosine = np.zeros((MAXLEN, LANES), np.float32)
    first = np.zeros((MAXLEN, LANES), np.float32)
    second = np.zeros((MAXLEN, LANES), np.float32)
    cosine[:, :120] = np.cos(angle)[:, place % 12]
    sines = np.sin(angle)[:, place % 12]
    first[:, :120] = np.where(place < 12, -sines, 0.0)
    second[:, :120] = np.where(place >= 12, sines, 0.0)
    low = lambda v: jnp.asarray(v.astype(jnp.bfloat16))
    return (low(squeeze), low(squeeze.T), low(spread), jnp.asarray(cosine), jnp.asarray(first), jnp.asarray(second))


LATE, EARLY = (0, 1, 2), (3, 4, 5)
ROUTES = (
    (0, 14, (0, 1, 3, 2, 4)),
    (14, 14, (0, 1, 2, 3, 4)),
    (28, 7, (2, 3, 0, 1, 4)),
    (35, 5, (0, 1, 3, 2, 4)),
    (40, 5, (0, 1, 2, 3, 4)),
    (45, 2, (2, 3, 0, 1, 4)),
)
GATHER_AT = (3, 14)
SCATTER_AT = (3, 12, 16, 19)


class Links:
    @staticmethod
    def scratch():
        n, tiles = len(ROUTES), (TILES, 16, LANES)
        bufs = [
            pltpu.VMEM((2,) * (4 - stage) + (count, 16, LANES), bf16)
            for begin, count, order in ROUTES
            for stage in range(5)
        ]
        return bufs + [
            pltpu.VMEM((2,) * 5 + tiles, bf16),
            pltpu.VMEM((2,) * 5 + tiles, bf16),
            pltpu.VMEM((5, 8, WIDE), f32),
            pltpu.VMEM((5, 8, WIDE), f32),
            pltpu.SemaphoreType.DMA,
            pltpu.SemaphoreType.DMA((n, 5)),
            pltpu.SemaphoreType.DMA((n, 5)),
            pltpu.SemaphoreType.DMA((n, 5)),
            pltpu.SemaphoreType.DMA((n, 5)),
            pltpu.SemaphoreType.DMA((5,)),
            pltpu.SemaphoreType.DMA((5,)),
        ]

    def __init__(self, shard, total, norm_total, *scratch):
        n = len(ROUTES)
        self.shard, self.total, self.norm_total = shard, total, norm_total
        self.bufs = [scratch[5 * r : 5 * r + 5] for r in range(n)]
        (
            self.whole, self.parts, self.norm_now, self.norm_in, self.own_sem,
            self.g_send, self.g_recv, self.s_send, self.s_recv, self.n_send, self.n_recv,
        ) = scratch[5 * n :]
        dp, tensor = lax.axis_index("dp"), lax.axis_index("tensor")
        self.coords = (dp // 4, (dp // 2) % 2, dp % 2, tensor // 2, tensor % 2)

    def partner(self, dim):
        c = list(self.coords)
        c[dim] = 1 - c[dim]
        return (c[0] * 4 + c[1] * 2 + c[2], c[3] * 2 + c[4])

    def greet(self):
        barrier = pltpu.get_barrier_semaphore()
        for dim in range(5):
            pl.semaphore_signal(barrier, inc=1, device_id=self.partner(dim), device_id_type=MESH)
        pl.semaphore_wait(barrier, 5)

    def keep_own(self):
        copy = pltpu.make_async_copy(self.shard, self.whole.at[self.coords], self.own_sem)
        copy.start()
        copy.wait()

    def gather_copy(self, r, stage):
        begin, count, order = ROUTES[r]
        done, dim = order[:stage], order[stage]
        where = tuple(slice(None) if d in done else self.coords[d] for d in range(5)) + (pl.ds(begin, count),)
        return pltpu.make_async_remote_copy(
            src_ref=self.whole.at[where],
            dst_ref=self.whole.at[where],
            send_sem=self.g_send.at[r, stage],
            recv_sem=self.g_recv.at[r, stage],
            device_id=self.partner(dim),
            device_id_type=MESH,
        )

    def gather_step(self, group, stage):
        for r in group:
            if stage > 0:
                self.gather_copy(r, stage - 1).wait_recv()
            if stage < 5:
                self.gather_copy(r, stage).start()

    def sums(self, r, stage, coordinate):
        begin, count, order = ROUTES[r]
        order = order[::-1]
        left = [d for d in range(5) if d not in order[:stage]]
        where = tuple(coordinate if d == order[stage] else slice(None) for d in left)
        if stage == 0:
            return self.parts.at[where + (pl.ds(begin, count),)]
        return self.bufs[r][stage - 1].at[where]

    def scatter_copy(self, r, stage):
        dim = ROUTES[r][2][4 - stage]
        return pltpu.make_async_remote_copy(
            src_ref=self.sums(r, stage, 1 - self.coords[dim]),
            dst_ref=self.bufs[r][stage],
            send_sem=self.s_send.at[r, stage],
            recv_sem=self.s_recv.at[r, stage],
            device_id=self.partner(dim),
            device_id_type=MESH,
        )

    def scatter_step(self, group, stage):
        for r in group:
            begin, count, order = ROUTES[r]
            if stage > 0:
                self.scatter_copy(r, stage - 1).wait_recv()
                buf = self.bufs[r][stage - 1]
                mine = self.sums(r, stage - 1, self.coords[order[5 - stage]])[...]
                if stage < 5:
                    buf[...] = buf[...] + mine
                else:
                    self.total[begin : begin + count] = buf[...].astype(f32) + mine.astype(f32)
            if stage < 5:
                self.scatter_copy(r, stage).start()

    def norm_copy(self, stage):
        return pltpu.make_async_remote_copy(
            src_ref=self.norm_now.at[stage],
            dst_ref=self.norm_in.at[stage],
            send_sem=self.n_send.at[stage],
            recv_sem=self.n_recv.at[stage],
            device_id=self.partner(stage),
            device_id_type=MESH,
        )

    def norm_start(self, values):
        self.norm_now[0] = values
        self.norm_copy(0).start()

    def norm_step(self, stage):
        self.norm_copy(stage).wait_recv()
        now = self.norm_now[stage] + self.norm_in[stage]
        if stage < 4:
            self.norm_now[stage + 1] = now
            self.norm_copy(stage + 1).start()
        else:
            self.norm_total[...] = now

    def finish(self):
        for stage in range(5):
            for r in range(len(ROUTES)):
                self.gather_copy(r, stage).wait_send()
                self.scatter_copy(r, stage).wait_send()
            self.norm_copy(stage).wait_send()


def gelu_parts(u):
    half = 0.5 * (1.0 + lax.erf(u * 0.7071067811865476))
    return u * half, half + u * jnp.exp(-0.5 * u * u) * 0.3989422804014327


def layer_kernel(remote, *refs):
    lengths, clusters, weights_of, source, tok, cot, norm, squeeze, widen, spread, cosine, first, second = refs[:13]
    layer_out, tokens_grad, G_out, norm_out = refs[13:17]
    (
        up_s, down_s, qkv_s, out_s, q_s, k_s, v_s, kT_s, vT_s, P_s, OT_s, att_s, dA_s, dqT_s, dk_s, dv_s,
        act1_s, act2_s, act_pad, plain1, plain2, res_s, y_s, dn_s, dres_s, dlow_s, eye_s, gdown_s, x_s,
    ) = refs[17:46]
    if remote:
        links = Links(source, G_out, norm_out, *refs[46:])
        W, G = links.whole, links.parts
        links.greet()
        links.keep_own()
        links.gather_step(EARLY, 0)
    else:
        links, W, G = None, source, G_out
    me = lax.axis_index("tensor")
    length = lengths[me]
    scale_row = weights_of[clusters[me]]
    scale = HEAD ** -0.5

    lane = lax.broadcasted_iota(jnp.int32, (1, WIDE), 1)
    real = jnp.where(lane < D, 1.0, 0.0)
    gains = norm[...]

    def norm_rows(values, gain, shift):
        middle = jnp.sum(values, axis=-1, keepdims=True) * (1.0 / D)
        centered = (values - middle) * real
        spread_ = jnp.sum(centered * centered, axis=-1, keepdims=True) * (1.0 / D)
        inverse = lax.rsqrt(spread_ + norm_eps)
        plain = centered * inverse
        return plain * gain + shift, plain, inverse

    def norm_back(dz, plain, inverse, gain):
        dg = jnp.sum(dz * plain, axis=0, keepdims=True)
        db = jnp.sum(dz, axis=0, keepdims=True)
        scaled = dz * gain
        one = jnp.sum(scaled, axis=-1, keepdims=True) * (1.0 / D)
        two = jnp.sum(scaled * plain, axis=-1, keepdims=True) * (1.0 / D)
        return inverse * (scaled - one - plain * two) * real, dg, db

    x_s[...] = jnp.zeros_like(x_s)
    x_s[:D, :] = tok[...].astype(f32)
    dres_s[...] = jnp.zeros_like(dres_s)
    dres_s[:D, :] = cot[...].astype(f32)
    x_s[...] = x_s[...].T
    normed, plain, inverse1 = norm_rows(x_s[...], gains[0:1], gains[1:2])
    plain1[...] = plain
    act1_s[...] = normed.astype(bf16)
    if remote:
        links.gather_step(EARLY, 1)
    row = lax.broadcasted_iota(jnp.int32, (MAXLEN, 1), 0)
    row_scale = jnp.where(row < length, scale_row, 0.0)
    dres_s[...] = dres_s[...].T * row_scale
    dlow_s[...] = dres_s[...].astype(bf16)
    if remote:
        links.gather_step(EARLY, 2)
        links.gather_step(LATE, 0)
        links.gather_step(EARLY, 3)
        links.gather_step(EARLY, 4)
        links.gather_step(LATE, 1)
        links.gather_step(EARLY, 5)
        links.gather_step(LATE, 2)

    for t in range(NTEN):
        mine = (slice(None),) * 3 + (t // 2, t % 2)
        pieces = [W[mine + (slice(QKV0 + 4 * c, QKV0 + 4 * c + 4),)].reshape(WIDE, LANES) for c in range(3)]
        plain = mm(squeeze[...], jnp.concatenate(pieces, 1)).astype(bf16)
        qkv_s[t] = mm(plain, spread[...]).astype(bf16)
    cosv, firstv, secondv = cosine[...], first[...], second[...]
    for t in range(NTEN):
        joined = mm(act1_s[...], qkv_s[t])
        for number in range(2):
            u = joined[:, number * LANES : (number + 1) * LANES]
            r = u * cosv + pltpu.roll(u, LANES - 12, 1) * firstv + pltpu.roll(u, 12, 1) * secondv
            if number == 0:
                q_s[t] = r.astype(bf16)
            else:
                k_s[t] = r.astype(bf16)
                kT_s[t] = r.T.astype(bf16)
        v = joined[:, 2 * LANES :]
        v_s[t] = v.astype(bf16)
        vT_s[t] = v.T.astype(bf16)

    lane_id = lax.broadcasted_iota(jnp.int32, (1, LANES), 1)
    row_id = lax.broadcasted_iota(jnp.int32, (LANES, 1), 0)
    key_id = lax.broadcasted_iota(jnp.int32, (MAXLEN, 1), 0)
    usable = key_id < length

    OT_s[...] = jnp.zeros_like(OT_s)

    def forward_head(h, carry):
        t = h // HEADS_DEV
        begin = (h - t * HEADS_DEV) * HEAD
        lanes = jnp.where((lane_id >= begin) & (lane_id < begin + HEAD), 1.0, 0.0).astype(bf16)
        rows = jnp.where((row_id >= begin) & (row_id < begin + HEAD), 1.0, 0.0).astype(bf16)
        keys = k_s[t] * lanes
        values = vT_s[t] * rows
        for b in range(MAXLEN // QB):
            cols = slice(b * QB, (b + 1) * QB)
            s = mm_nt(keys, q_s[t, cols, :])
            s = jnp.where(usable, s * scale, masked_score)
            top = jnp.max(s, axis=0, keepdims=True)
            e = jnp.exp(s - top)
            total = jnp.sum(e, axis=0, keepdims=True)
            p = (e * (1.0 / total)).astype(bf16)
            P_s[h, :, cols] = p
            OT_s[t, :, cols] += mm(values, p)
        if remote:
            for number, when in enumerate(GATHER_AT):
                pl.when(h == when)(functools.partial(links.gather_step, LATE, 3 + number))
        return carry

    lax.fori_loop(0, NTEN * HEADS_DEV, forward_head, 0)

    if remote:
        links.gather_step(LATE, 5)
    res = x_s[...]
    for t in range(NTEN):
        mine = (slice(None),) * 3 + (t // 2, t % 2)
        pieces = [W[mine + (OUT0 + c,)].reshape(LANES, LANES) for c in range(4)]
        out_s[t] = mm(squeeze[:LANES, :LANES], jnp.concatenate(pieces, 1)).astype(bf16)
        att_s[t] = OT_s[t].T.astype(bf16)
        res = res + mm(att_s[t], out_s[t])
    res_s[...] = res
    normed, plain, inverse2 = norm_rows(res, gains[2:3], gains[3:4])
    plain2[...] = plain
    act2_s[...] = normed.astype(bf16)
    act_pad[...] = mm_nt(widen[...], act2_s[...]).astype(bf16)

    for c in range(15):
        part = mm(squeeze[...], W[:, :, :, :, :, UP0 + c].reshape(WIDE, LANES)).astype(bf16)
        up_s[:, c * LANES : (c + 1) * LANES] = part

    def down_rows(k, carry):
        mine = (k // 4, (k // 2) % 2, k % 2)
        pieces = [W[mine + (slice(None),) * 2 + (slice(DOWN0 + 4 * c, DOWN0 + 4 * c + 4),)].reshape(256, LANES) for c in range(4)]
        part = mm(squeeze[:240, :256], jnp.concatenate(pieces, 1)).astype(bf16)
        down_s[pl.ds(pl.multiple_of(k * 240, 16), 240), :] = part
        return carry

    lax.fori_loop(0, NDP, down_rows, 0)

    y_s[...] = res_s[...]
    dn_s[...] = jnp.zeros_like(dn_s)
    eye_row = lax.broadcasted_iota(jnp.int32, (CHUNK, CHUNK), 0)
    eye_col = lax.broadcasted_iota(jnp.int32, (CHUNK, CHUNK), 1)
    eye = jnp.where(eye_row == eye_col, 1.0, 0.0).astype(bf16)
    eye_s[...] = eye

    def hidden_chunk(c, carry):
        cols = pl.ds(pl.multiple_of(c * CHUNK, LANES), CHUNK)
        u = mm(act2_s[...], up_s[:, cols])
        value, slope = gelu_parts(u)
        a = value.astype(bf16)
        y_s[...] += mm(a, down_s[cols, :])
        d_active = mm_nt(dlow_s[...], down_s[cols, :])
        d_upper = (d_active * slope).astype(bf16)
        dn_s[...] += mm_nt(d_upper, up_s[:, cols])
        g_up = mm(act_pad[...], d_upper).astype(bf16)
        for part in range(3):
            G[:, :, :, :, :, UP0 + 3 * c + part] = g_up[:, part * LANES : (part + 1) * LANES].reshape(2, 2, 2, 2, 2, 16, LANES)
        aT = mm_nt(eye_s[...], a).astype(bf16)
        gdown_s[cols, :] = mm(aT, dlow_s[...]).astype(bf16)
        return carry

    lax.fori_loop(0, FF // CHUNK, hidden_chunk, 0)
    y_s[...] = y_s[...].T
    layer_out[...] = y_s[:D, :]

    def down_groups(k, carry):
        part = mm(widen[:256, :240], gdown_s[pl.ds(pl.multiple_of(k * 240, 16), 240), :]).astype(bf16)
        mine = (k // 4, (k // 2) % 2, k % 2)
        for c in range(4):
            where = mine + (slice(None),) * 2 + (slice(DOWN0 + 4 * c, DOWN0 + 4 * c + 4),)
            G[where] = part[:, c * LANES : (c + 1) * LANES].reshape(2, 2, 4, 16, LANES)
        return carry

    lax.fori_loop(0, 8, down_groups, 0)

    d_from, dg2, db2 = norm_back(dn_s[...], plain2[...], inverse2, gains[2:3])
    d_res = dres_s[...] + d_from
    dres_s[...] = d_res
    dlow_s[...] = d_res.astype(bf16)

    for t in range(NTEN):
        dA_s[t] = mm_nt(dlow_s[...], out_s[t]).astype(bf16)
        attT = mm_nt(widen[:LANES, :LANES], att_s[t]).astype(bf16)
        part = mm(attT, dlow_s[...]).astype(bf16)
        mine = (slice(None),) * 3 + (t // 2, t % 2)
        for c in range(4):
            G[mine + (OUT0 + c,)] = part[:, c * LANES : (c + 1) * LANES].reshape(2, 2, 2, 16, LANES)
    if remote:
        links.scatter_step(LATE, 0)

    dqT_s[...] = jnp.zeros_like(dqT_s)
    dk_s[...] = jnp.zeros_like(dk_s)
    dv_s[...] = jnp.zeros_like(dv_s)

    def backward_head(h, carry):
        t = h // HEADS_DEV
        begin = (h - t * HEADS_DEV) * HEAD
        lanes = jnp.where((lane_id >= begin) & (lane_id < begin + HEAD), 1.0, 0.0).astype(bf16)
        rows = jnp.where((row_id >= begin) & (row_id < begin + HEAD), 1.0, 0.0).astype(bf16)
        values = v_s[t]
        keysT = kT_s[t] * rows
        for b in range(MAXLEN // QB):
            cols = slice(b * QB, (b + 1) * QB)
            dA = dA_s[t, cols, :] * lanes
            dP = mm_nt(values, dA)
            low = P_s[h, :, cols]
            p = low.astype(f32)
            centre = jnp.sum(p * dP, axis=0, keepdims=True)
            ds = (p * (dP - centre)).astype(bf16)
            dv_s[t] += mm(low, dA)
            dk_s[t] += mm(ds, q_s[t, cols, :] * lanes)
            dqT_s[t, :, cols] += mm(keysT, ds)
        if remote:
            for number, when in enumerate(SCATTER_AT):
                pl.when(h == when)(functools.partial(links.scatter_step, LATE, 1 + number))
        return carry

    lax.fori_loop(0, NTEN * HEADS_DEV, backward_head, 0)

    act_pad[...] = mm_nt(widen[...], act1_s[...]).astype(bf16)
    for t in range(NTEN):
        pieces = []
        for number in range(2):
            g = (dqT_s[t].T if number == 0 else dk_s[t]) * scale
            r = g * cosv - pltpu.roll(g, LANES - 12, 1) * firstv - pltpu.roll(g, 12, 1) * secondv
            pieces.append(r.astype(bf16))
        pieces.append(dv_s[t].astype(bf16))
        d_joined = jnp.concatenate(pieces, 1)
        q_s[t], k_s[t], v_s[t] = pieces
        natural = mm_nt(d_joined, spread[...]).astype(bf16)
        part = mm(act_pad[...], natural).astype(bf16)
        mine = (slice(None),) * 3 + (t // 2, t % 2)
        for c in range(3):
            where = mine + (slice(QKV0 + 4 * c, QKV0 + 4 * c + 4),)
            G[where] = part[:, c * LANES : (c + 1) * LANES].reshape(2, 2, 2, 4, 16, LANES)
    if remote:
        links.scatter_step(EARLY, 0)
        links.scatter_step(LATE, 5)
    dz = jnp.zeros((MAXLEN, WIDE), f32)
    for t in range(NTEN):
        for number, ref in enumerate((q_s, k_s, v_s)):
            dz = dz + mm_nt(ref[t], qkv_s[t, :, number * LANES : (number + 1) * LANES])
    d_from, dg1, db1 = norm_back(dz, plain1[...], inverse1, gains[0:1])
    norm_parts = jnp.concatenate([dg1, db1, dg2, db2, jnp.zeros((4, WIDE), f32)], 0)
    if remote:
        links.norm_start(norm_parts)
        links.scatter_step(EARLY, 1)
    else:
        norm_out[...] = norm_parts
    x_s[...] = (dres_s[...] + d_from).T
    tokens_grad[...] = x_s[:D, :]
    if remote:
        for stage in range(5):
            if stage > 0:
                links.scatter_step(EARLY, stage + 1)
            links.norm_step(stage)
        links.finish()


def run_layer(lengths, clusters, cluster_weight, source, tokens, cotangent, norm_master, remote):
    rows = MAXLEN
    wide_norm = jnp.pad(norm_master, ((0, 0), (0, WIDE - D)))
    smem = pl.BlockSpec(memory_space=pltpu.SMEM)
    vmem = pl.BlockSpec(memory_space=pltpu.VMEM)
    head_set = (NTEN, MAXLEN, LANES)
    turned = (NTEN, LANES, MAXLEN)
    wide = (rows, WIDE)
    scratch = [
        pltpu.VMEM((WIDE, FF), bf16),
        pltpu.VMEM((FF, WIDE), bf16),
        pltpu.VMEM((NTEN, WIDE, CHUNK), bf16),
        pltpu.VMEM((NTEN, LANES, WIDE), bf16),
        pltpu.VMEM(head_set, bf16),
        pltpu.VMEM(head_set, bf16),
        pltpu.VMEM(head_set, bf16),
        pltpu.VMEM(turned, bf16),
        pltpu.VMEM(turned, bf16),
        pltpu.VMEM((NTEN * HEADS_DEV, MAXLEN, MAXLEN), bf16),
        pltpu.VMEM(turned, f32),
        pltpu.VMEM(head_set, bf16),
        pltpu.VMEM(head_set, bf16),
        pltpu.VMEM(turned, f32),
        pltpu.VMEM(head_set, f32),
        pltpu.VMEM(head_set, f32),
        pltpu.VMEM(wide, bf16),
        pltpu.VMEM(wide, bf16),
        pltpu.VMEM(wide, bf16),
        pltpu.VMEM(wide, f32),
        pltpu.VMEM(wide, f32),
        pltpu.VMEM(wide, f32),
        pltpu.VMEM(wide, f32),
        pltpu.VMEM(wide, f32),
        pltpu.VMEM(wide, f32),
        pltpu.VMEM(wide, bf16),
        pltpu.VMEM((CHUNK, CHUNK), bf16),
        pltpu.VMEM((FF, WIDE), bf16),
        pltpu.VMEM(wide, f32),
    ]
    tiles = (TILES, 16, LANES)
    params = dict(vmem_limit_bytes=66_900_000)
    if remote:
        result = jax.ShapeDtypeStruct(tiles, f32)
        scratch += Links.scratch()
        params.update(collective_id=0, has_side_effects=True)
    else:
        result = jax.ShapeDtypeStruct((2,) * 5 + tiles, bf16)
        source = source.reshape((2,) * 5 + tiles)
    turned_out, turned_grad, grads, norm_grad = pl.pallas_call(
        functools.partial(layer_kernel, remote),
        out_shape=(
            jax.ShapeDtypeStruct((D, rows), f32),
            jax.ShapeDtypeStruct((D, rows), f32),
            result,
            jax.ShapeDtypeStruct((8, WIDE), f32),
        ),
        in_specs=[smem] * 3 + [vmem] * 10,
        out_specs=[vmem] * 4,
        scratch_shapes=scratch,
        compiler_params=pltpu.CompilerParams(**params),
        name="layer",
    )(lengths, clusters, cluster_weight, source, tokens.T, cotangent.T, wide_norm, *constants())
    if not remote:
        grads = grads.reshape(NDP, NTEN, *tiles)
    return turned_out.T, turned_grad.T, grads, norm_grad


def shard_tiles(up, down, qkv, out):
    up = jnp.pad(up.reshape(15, 15, LANES), ((0, 1), (0, 0), (0, 0))).transpose(1, 0, 2)
    down = jnp.pad(down.reshape(4, 15, D), ((0, 0), (0, 1), (0, WIDE - D)))
    down = down.reshape(4, 16, 4, LANES).transpose(2, 0, 1, 3).reshape(16, 16, LANES)
    qkv = jnp.pad(qkv.reshape(4, 15, 360), ((0, 0), (0, 1), (0, CHUNK - 360)))
    qkv = qkv.reshape(4, 16, 3, LANES).transpose(2, 0, 1, 3).reshape(12, 16, LANES)
    out = jnp.pad(out.reshape(15, D), ((0, 1), (0, WIDE - D)))
    out = out.reshape(16, 4, LANES).transpose(1, 0, 2)
    return jnp.concatenate([up, down, out, qkv], 0)


def tiles_shard(tiles):
    up = tiles[UP0:DOWN0, :15].transpose(1, 0, 2).reshape(-1)
    down = tiles[DOWN0:OUT0].reshape(4, 4, 16, LANES).transpose(1, 2, 0, 3)[:, :15].reshape(60, WIDE)[:, :D].reshape(-1)
    qkv = tiles[QKV0:].reshape(3, 4, 16, LANES).transpose(1, 2, 0, 3)[:, :15].reshape(60, CHUNK)[:, :360].reshape(1, -1)
    out = tiles[OUT0:QKV0].transpose(1, 0, 2)[:15].reshape(15, WIDE)[:, :D].reshape(1, -1)
    return up, down, qkv, out


def adam_step(master, moment, square, average, grad, rate):
    moment_new = beta_one * moment + (1.0 - beta_one) * grad
    square_new = beta_two * square + (1.0 - beta_two) * grad * grad
    update = moment_new / (jnp.sqrt(square_new) + adam_eps) + decay_rate * master
    fresh = master - rate * update
    average_new = average_keep * average + (1.0 - average_keep) * fresh
    return (fresh, moment_new, square_new, average_new)


def to_groups(up, down, qkv, out):
    up, down = up.reshape(NDP, NTEN, -1), down.reshape(NDP, NTEN, -1)
    qkv = qkv.reshape(NTEN, NDP, -1).transpose(1, 0, 2)
    out = out.reshape(NTEN, NDP, -1).transpose(1, 0, 2)
    return jax.vmap(jax.vmap(shard_tiles))(up, down, qkv, out)


def from_groups(tiles):
    up, down, qkv, out = jax.vmap(jax.vmap(tiles_shard))(tiles.astype(f32))
    qkv = qkv.reshape(NDP, NTEN, -1).transpose(1, 0, 2).reshape(NTEN, -1)
    out = out.reshape(NDP, NTEN, -1).transpose(1, 0, 2).reshape(NTEN, -1)
    return up.reshape(-1), down.reshape(-1), qkv, out


def on_device(tokens, cotangent, lengths, clusters, cluster_weight, *state):
    qkv, out, up, down, norm = (state[4 * k : 4 * k + 4] for k in range(5))
    ends = ("dp", "tensor")
    low = tuple(w[0].astype(bf16) for w in (up, down, qkv, out))
    grid = (lax.axis_size("dp"), lax.axis_size("tensor")) == (NDP, NTEN)
    if grid:
        source = shard_tiles(*low)
    else:
        whole = [lax.all_gather(w, ends, axis=0, tiled=True) for w in low[:2]]
        for w in low[2:]:
            block = lax.all_gather(w, "dp", axis=1, tiled=True)
            whole.append(lax.all_gather(block, "tensor", axis=0, tiled=True))
        source = to_groups(*whole)
    layer_out, tokens_grad, total, norm_total = run_layer(
        lengths, clusters, cluster_weight, source, tokens, cotangent, norm[0], grid
    )
    if grid:
        grads = tiles_shard(total)
    else:
        whole = from_groups(total)
        grads = [lax.psum_scatter(g, ends, scatter_dimension=0, tiled=True) for g in whole[:2]]
        for g in whole[2:]:
            block = lax.psum_scatter(g, "tensor", scatter_dimension=0, tiled=True)
            grads.append(lax.psum_scatter(block, "dp", scatter_dimension=1, tiled=True))
        norm_total = lax.psum(norm_total, ends)
    up_grad, down_grad, qkv_grad, out_grad = grads
    results = (layer_out, tokens_grad)
    results += adam_step(*qkv, qkv_grad, D ** (-0.5))
    results += adam_step(*out, out_grad, (D // 32) ** (-0.5))
    results += adam_step(*up, up_grad, D ** (-0.5))
    results += adam_step(*down, down_grad, FF ** (-0.5))
    results += adam_step(*norm, norm_total[:4, :D], 0.2)
    return results


def solution(mesh):
    rows, both, flat = P(("dp", "tensor"), None), P("tensor", "dp"), P(("dp", "tensor"))
    state = (both,) * 8 + (flat,) * 8 + (P(),) * 4
    return jax.shard_map(
        on_device,
        mesh=mesh,
        in_specs=(rows, rows, P("dp"), P("dp"), P()) + state,
        out_specs=(rows, rows) + state,
        check_vma=False,
    )
```

```python
import functools

import jax
import jax.numpy as jnp
import numpy as np
from jax import lax
from jax.experimental import pallas as pl
from jax.experimental.pallas import tpu as pltpu
from jax.sharding import PartitionSpec as P

D = 480
HEAD = 24
FF = 1920
MAXLEN = 512
NDP, NTEN = 8, 4
WIDE = 512
HEADS_DEV = 5
LANES = 128
TILES = 47
JOINED = 1536
UP0, OUT0, DOWN0, QKV0 = 0, 15, 19, 35
CHUNK = 384
QB = 512
SPARE = 120

norm_eps = 1e-05
beta_one = 0.5
beta_two = 0.5
adam_eps = 1e-08
decay_rate = 0.01
average_keep = 0.75
hidden_score = -1e38
MESH = pl.DeviceIdType.MESH
f32, bf16 = jnp.float32, jnp.bfloat16


def mm(a, b):
    return lax.dot_general(a, b, (((1,), (0,)), ((), ())), preferred_element_type=f32)


def mm_nt(a, b):
    return lax.dot_general(a, b, (((1,), (1,)), ((), ())), preferred_element_type=f32)


def constants():
    natural = np.arange(D)
    squeeze = np.zeros((WIDE, WIDE), np.float32)
    squeeze[natural, 16 * (natural // 15) + natural % 15] = 1.0
    position = np.arange(MAXLEN, dtype=np.float32)
    exponent = np.arange(HEAD // 2, dtype=np.float32) * np.float32(2.0 / HEAD)
    inverse = np.float32(10000.0) ** (-exponent)
    angle = (position[:, None] * inverse[None, :]).astype(np.float32).astype(np.float64)
    lane = np.arange(120)
    place = lane % HEAD
    cosine = np.zeros((MAXLEN, LANES), np.float32)
    first = np.zeros((MAXLEN, LANES), np.float32)
    second = np.zeros((MAXLEN, LANES), np.float32)
    cosine[:, :120] = np.cos(angle)[:, place % 12]
    sines = np.sin(angle)[:, place % 12]
    first[:, :120] = np.where(place < 12, -sines, 0.0)
    second[:, :120] = np.where(place >= 12, sines, 0.0)
    low = lambda v: jnp.asarray(v.astype(jnp.bfloat16))
    return (low(squeeze), low(squeeze.T), jnp.asarray(cosine), jnp.asarray(first), jnp.asarray(second))


UP, DOWN, EARLY = (0, 1, 2), (3, 4, 5), (6, 7, 8)
WAY_A, WAY_B, WAY_C = (0, 1, 3, 2, 4), (0, 1, 2, 3, 4), (2, 3, 0, 1, 4)
GATHER_ROUTES = (
    (0, 8, WAY_A), (8, 8, WAY_B), (16, 3, WAY_C),
    (19, 6, WAY_A), (25, 7, WAY_B), (32, 3, WAY_C),
    (35, 5, WAY_A), (40, 5, WAY_B), (45, 2, WAY_C),
)
SCATTER_ROUTES = (
    (0, 6, WAY_A), (6, 6, WAY_B), (12, 3, WAY_C),
    (15, 8, WAY_A), (23, 8, WAY_B), (31, 4, WAY_C),
    (35, 5, WAY_A), (40, 5, WAY_B), (45, 2, WAY_C),
)
GATHER_AT = ((1, DOWN, 1), (3, UP, 3), (5, DOWN, 2), (10, UP, 4), (11, DOWN, 3), (18, DOWN, 4))
SCATTER_AT = ((3, UP, 2), (4, DOWN, 1), (8, UP, 3), (10, DOWN, 2), (11, UP, 4), (14, DOWN, 3), (17, DOWN, 4))


class Links:
    @staticmethod
    def scratch():
        n, tiles = len(SCATTER_ROUTES), (TILES, 16, LANES)
        bufs = [
            pltpu.VMEM((2,) * (4 - stage) + (count, 16, LANES), bf16)
            for begin, count, order in SCATTER_ROUTES
            for stage in range(5)
        ]
        return bufs + [
            pltpu.VMEM((2,) * 5 + tiles, bf16),
            pltpu.VMEM((2,) * 5 + tiles, bf16),
            pltpu.VMEM((3, 8, WIDE), f32),
            pltpu.VMEM((3, 4, 8, WIDE), f32),
            pltpu.SemaphoreType.DMA,
            pltpu.SemaphoreType.DMA((n, 5)),
            pltpu.SemaphoreType.DMA((n, 5)),
            pltpu.SemaphoreType.DMA((n, 5)),
            pltpu.SemaphoreType.DMA((n, 5)),
            pltpu.SemaphoreType.DMA((3, 3)),
            pltpu.SemaphoreType.DMA((3, 3)),
        ]

    def __init__(self, shard, total, norm_total, *scratch):
        n = len(SCATTER_ROUTES)
        self.shard, self.total, self.norm_total = shard, total, norm_total
        self.bufs = [scratch[5 * r : 5 * r + 5] for r in range(n)]
        (
            self.whole, self.parts, self.norm_now, self.norm_in, self.own_sem,
            self.g_send, self.g_recv, self.s_send, self.s_recv, self.n_send, self.n_recv,
        ) = scratch[5 * n :]
        dp, tensor = lax.axis_index("dp"), lax.axis_index("tensor")
        self.coords = (dp // 4, (dp // 2) % 2, dp % 2, tensor // 2, tensor % 2)

    def partner(self, dim):
        c = list(self.coords)
        c[dim] = 1 - c[dim]
        return (c[0] * 4 + c[1] * 2 + c[2], c[3] * 2 + c[4])

    def peers(self, group):
        z0, z1, x, y, core = self.coords
        found = []
        if group == 0:
            mine = z0 * 2 + z1
            for step in range(1, 4):
                z = (mine + step) % 4
                found.append(((z * 2 + x, y * 2 + core), z))
        elif group == 1:
            mine = x * 2 + y
            for dx, dy in ((0, 1), (1, 0), (1, 1)):
                px, py = (x + dx) % 2, (y + dy) % 2
                found.append((((z0 * 2 + z1) * 2 + px, py * 2 + core), px * 2 + py))
        else:
            mine = core
            found.append((((z0 * 2 + z1) * 2 + x, y * 2 + 1 - core), 1 - core))
        return found, mine

    def greet(self):
        barrier = pltpu.get_barrier_semaphore()
        others = [device for group in range(3) for device, slot in self.peers(group)[0]]
        for device in others:
            pl.semaphore_signal(barrier, inc=1, device_id=device, device_id_type=MESH)
        pl.semaphore_wait(barrier, len(others))

    def keep_own(self):
        copy = pltpu.make_async_copy(self.shard, self.whole.at[self.coords], self.own_sem)
        copy.start()
        copy.wait()

    def gather_copy(self, r, stage):
        begin, count, order = GATHER_ROUTES[r]
        done, dim = order[:stage], order[stage]
        where = tuple(slice(None) if d in done else self.coords[d] for d in range(5)) + (pl.ds(begin, count),)
        return pltpu.make_async_remote_copy(
            src_ref=self.whole.at[where],
            dst_ref=self.whole.at[where],
            send_sem=self.g_send.at[r, stage],
            recv_sem=self.g_recv.at[r, stage],
            device_id=self.partner(dim),
            device_id_type=MESH,
        )

    def gather_step(self, group, stage):
        for r in group:
            if stage > 0:
                self.gather_copy(r, stage - 1).wait_recv()
            if stage < 5:
                self.gather_copy(r, stage).start()

    def sums(self, r, stage, coordinate):
        begin, count, order = SCATTER_ROUTES[r]
        order = order[::-1]
        left = [d for d in range(5) if d not in order[:stage]]
        where = tuple(coordinate if d == order[stage] else slice(None) for d in left)
        if stage == 0:
            return self.parts.at[where + (pl.ds(begin, count),)]
        return self.bufs[r][stage - 1].at[where]

    def scatter_copy(self, r, stage):
        dim = SCATTER_ROUTES[r][2][4 - stage]
        return pltpu.make_async_remote_copy(
            src_ref=self.sums(r, stage, 1 - self.coords[dim]),
            dst_ref=self.bufs[r][stage],
            send_sem=self.s_send.at[r, stage],
            recv_sem=self.s_recv.at[r, stage],
            device_id=self.partner(dim),
            device_id_type=MESH,
        )

    def scatter_step(self, group, stage):
        for r in group:
            begin, count, order = SCATTER_ROUTES[r]
            if stage > 0:
                self.scatter_copy(r, stage - 1).wait_recv()
                buf = self.bufs[r][stage - 1]
                mine = self.sums(r, stage - 1, self.coords[order[5 - stage]])[...]
                if stage < 5:
                    buf[...] = buf[...] + mine
                else:
                    self.total[begin : begin + count] = buf[...].astype(f32) + mine.astype(f32)
            if stage < 5:
                self.scatter_copy(r, stage).start()

    def norm_copies(self, group):
        found, mine = self.peers(group)
        return [
            pltpu.make_async_remote_copy(
                src_ref=self.norm_now.at[group],
                dst_ref=self.norm_in.at[group, mine],
                send_sem=self.n_send.at[group, k],
                recv_sem=self.n_recv.at[group, k],
                device_id=device,
                device_id_type=MESH,
            )
            for k, (device, slot) in enumerate(found)
        ]

    def norm_start(self, values, group=0):
        self.norm_now[group] = values
        self.norm_in[group, self.peers(group)[1]] = values
        for copy in self.norm_copies(group):
            copy.start()

    def norm_step(self, group):
        for copy in self.norm_copies(group):
            copy.wait_recv()
        now = self.norm_in[group, 0]
        for slot in range(1, 2 if group == 2 else 4):
            now = now + self.norm_in[group, slot]
        if group < 2:
            self.norm_start(now, group + 1)
        else:
            self.norm_total[...] = now

    def finish(self):
        for stage in range(5):
            for r in range(len(GATHER_ROUTES)):
                self.gather_copy(r, stage).wait_send()
            for r in range(len(SCATTER_ROUTES)):
                self.scatter_copy(r, stage).wait_send()
        for group in range(3):
            for copy in self.norm_copies(group):
                copy.wait_send()


def gelu_parts(u):
    half = 0.5 * (1.0 + lax.erf(u * 0.7071067811865476))
    return u * half, half + u * jnp.exp(-0.5 * u * u) * 0.3989422804014327


def layer_kernel(remote, *refs):
    lengths, clusters, weights_of, source, tok, cot, norm, squeeze, widen, cosine, first, second = refs[:12]
    layer_out, tokens_grad, G_out, norm_out = refs[12:16]
    (
        up_s, down_s, qkv_s, dj_s, out_s, q_s, k_s, v_s, kT_s, vT_s, P_s, OT_s, att_s, dA_s, dqT_s, dk_s, dv_s,
        act1_s, act2_s, act_pad, plain1, plain2, res_s, y_s, dn_s, dres_s, dlow_s, eye_s, x_s, centre_s, ds_s, act_pad1,
    ) = refs[16:48]
    if remote:
        links = Links(source, G_out, norm_out, *refs[48:])
        W, G = links.whole, links.parts
        links.greet()
        links.keep_own()
        links.gather_step(EARLY, 0)
    else:
        links, W, G = None, source, G_out
    me = lax.axis_index("tensor")
    length = lengths[me]
    scale_row = weights_of[clusters[me]]
    scale = HEAD ** -0.5

    lane = lax.broadcasted_iota(jnp.int32, (1, WIDE), 1)
    real = jnp.where(lane < D, 1.0, 0.0)
    gains = norm[...]

    def norm_rows(values, gain, shift):
        middle = jnp.sum(values, axis=-1, keepdims=True) * (1.0 / D)
        centered = (values - middle) * real
        spread_ = jnp.sum(centered * centered, axis=-1, keepdims=True) * (1.0 / D)
        inverse = lax.rsqrt(spread_ + norm_eps)
        plain = centered * inverse
        return plain * gain + shift, plain, inverse

    def norm_back(dz, plain, inverse, gain):
        dg = jnp.sum(dz * plain, axis=0, keepdims=True)
        db = jnp.sum(dz, axis=0, keepdims=True)
        scaled = dz * gain
        one = jnp.sum(scaled, axis=-1, keepdims=True) * (1.0 / D)
        two = jnp.sum(scaled * plain, axis=-1, keepdims=True) * (1.0 / D)
        return inverse * (scaled - one - plain * two) * real, dg, db

    x_s[...] = jnp.zeros_like(x_s)
    x_s[:D, :] = tok[...].astype(f32)
    dres_s[...] = jnp.zeros_like(dres_s)
    dres_s[:D, :] = cot[...].astype(f32)
    x_s[...] = x_s[...].T
    normed, plain, inverse1 = norm_rows(x_s[...], gains[0:1], gains[1:2])
    plain1[...] = plain
    act1_s[...] = normed.astype(bf16)
    if remote:
        links.gather_step(EARLY, 1)
    row = lax.broadcasted_iota(jnp.int32, (MAXLEN, 1), 0)
    row_scale = jnp.where(row < length, scale_row, 0.0)
    dres_s[...] = dres_s[...].T * row_scale
    dlow_s[...] = dres_s[...].astype(bf16)
    act_pad1[...] = mm_nt(widen[...], act1_s[...]).astype(bf16)
    if remote:
        links.gather_step(EARLY, 2)
        links.gather_step(UP, 0)
        links.gather_step(EARLY, 3)
        links.gather_step(EARLY, 4)
        links.gather_step(UP, 1)
        links.gather_step(EARLY, 5)
        links.gather_step(UP, 2)
        links.gather_step(DOWN, 0)

    for pair in range(2):
        pieces = []
        for t in (2 * pair, 2 * pair + 1):
            mine = (slice(None),) * 3 + (t // 2, t % 2)
            pieces += [W[mine + (slice(QKV0 + 4 * c, QKV0 + 4 * c + 4),)].reshape(WIDE, LANES) for c in range(3)]
        half = slice(pair * (JOINED // 2), (pair + 1) * (JOINED // 2))
        qkv_s[:, half] = mm(squeeze[...], jnp.concatenate(pieces, 1)).astype(bf16)
    cosv, firstv, secondv = cosine[...], first[...], second[...]
    lane_id = lax.broadcasted_iota(jnp.int32, (1, LANES), 1)
    key_id = lax.broadcasted_iota(jnp.int32, (MAXLEN, 1), 0)
    spare = jnp.where(lane_id == SPARE, 1.0, 0.0)
    key_bias = jnp.where(key_id < length, 0.0, hidden_score) * spare

    def strided(block):
        gap = jnp.zeros((8, MAXLEN), f32)
        return jnp.concatenate([x for j in range(HEADS_DEV) for x in (block[j * HEAD : (j + 1) * HEAD], gap)], 0)

    def dense(block):
        rows = [block[j * 32 : j * 32 + HEAD] for j in range(HEADS_DEV)]
        return jnp.concatenate(rows + [jnp.zeros((8, MAXLEN), f32)], 0)

    for t in range(NTEN):
        if t % 2 == 0:
            both = mm(act1_s[...], qkv_s[:, t * 3 * LANES : (t + 2) * 3 * LANES])
        joined = both[:, (t % 2) * 3 * LANES : (t % 2 + 1) * 3 * LANES]
        for number in range(2):
            u = joined[:, number * LANES : (number + 1) * LANES]
            r = u * cosv + pltpu.roll(u, LANES - 12, 1) * firstv + pltpu.roll(u, 12, 1) * secondv
            if number == 0:
                q_s[t] = (r + spare).astype(bf16)
            else:
                k_s[t] = (r + key_bias).astype(bf16)
                kT_s[t] = strided(r.T).astype(bf16)
        v = joined[:, 2 * LANES :]
        v_s[t] = v.astype(bf16)
        vT_s[t] = strided(v.T).astype(bf16)

    fold = HEAD ** -0.5 * 1.4426950408889634

    def forward_head(h, carry):
        t = h // HEADS_DEV
        j = h - t * HEADS_DEV
        begin = j * HEAD
        kept = ((lane_id >= begin) & (lane_id < begin + HEAD)) | (lane_id == SPARE)
        keys = k_s[t] * jnp.where(kept, 1.0, 0.0).astype(bf16)
        rows = pl.ds(pl.multiple_of(j * 32, 32), 32)
        values = vT_s[t, rows, :]
        for b in range(MAXLEN // QB):
            cols = slice(b * QB, (b + 1) * QB)
            s = mm_nt(keys, q_s[t, cols, :])
            top = jnp.max(s, axis=0, keepdims=True)
            e = jnp.exp2(s * fold - top * fold)
            total = jnp.sum(e, axis=0, keepdims=True)
            p = (e * (1.0 / total)).astype(bf16)
            P_s[h, :, cols] = p
            OT_s[t, rows, cols] = mm(values, p)
        if remote:
            for when, group, number in GATHER_AT:
                pl.when(h == when)(functools.partial(links.gather_step, group, number))
        return carry

    lax.fori_loop(0, NTEN * HEADS_DEV, forward_head, 0)

    if remote:
        links.gather_step(UP, 5)
    res = x_s[...]
    for t in range(NTEN):
        mine = (slice(None),) * 3 + (t // 2, t % 2)
        pieces = [W[mine + (OUT0 + c,)].reshape(LANES, LANES) for c in range(4)]
        out_s[t] = mm(squeeze[:LANES, :LANES], jnp.concatenate(pieces, 1)).astype(bf16)
        att_s[t] = dense(OT_s[t]).T.astype(bf16)
        res = res + mm(att_s[t], out_s[t])
    res_s[...] = res
    normed, plain, inverse2 = norm_rows(res, gains[2:3], gains[3:4])
    plain2[...] = plain
    act2_s[...] = normed.astype(bf16)
    act_pad[...] = mm_nt(widen[...], act2_s[...]).astype(bf16)

    for c in range(8):
        pieces = [W[:, :, :, :, :, UP0 + n].reshape(WIDE, LANES) for n in range(2 * c, min(2 * c + 2, 15))]
        up_s[:, 2 * c * LANES : (2 * c + len(pieces)) * LANES] = mm(squeeze[...], jnp.concatenate(pieces, 1)).astype(bf16)

    if remote:
        links.gather_step(DOWN, 5)

    def down_rows(k, carry):
        mine = (k // 4, (k // 2) % 2, k % 2)
        pieces = [W[mine + (slice(None),) * 2 + (slice(DOWN0 + 4 * c, DOWN0 + 4 * c + 4),)].reshape(256, LANES) for c in range(4)]
        part = mm(squeeze[:240, :256], jnp.concatenate(pieces, 1)).astype(bf16)
        down_s[pl.ds(pl.multiple_of(k * 240, 16), 240), :] = part
        return carry

    lax.fori_loop(0, NDP, down_rows, 0)

    y_s[...] = res_s[...]
    dn_s[...] = jnp.zeros_like(dn_s)
    eye_row = lax.broadcasted_iota(jnp.int32, (CHUNK, CHUNK), 0)
    eye_col = lax.broadcasted_iota(jnp.int32, (CHUNK, CHUNK), 1)
    eye = jnp.where(eye_row == eye_col, 1.0, 0.0).astype(bf16)
    eye_s[...] = eye

    def hidden_chunk(c, carry):
        cols = pl.ds(pl.multiple_of(c * CHUNK, LANES), CHUNK)
        u = mm(act2_s[...], up_s[:, cols])
        value, slope = gelu_parts(u)
        a = value.astype(bf16)
        y_s[...] += mm(a, down_s[cols, :])
        d_active = mm_nt(dlow_s[...], down_s[cols, :])
        d_upper = (d_active * slope).astype(bf16)
        dn_s[...] += mm_nt(d_upper, up_s[:, cols])
        g_up = mm(act_pad[...], d_upper).astype(bf16)
        for part in range(3):
            G[:, :, :, :, :, UP0 + 3 * c + part] = g_up[:, part * LANES : (part + 1) * LANES].reshape(2, 2, 2, 2, 2, 16, LANES)
        aT = mm_nt(eye_s[...], a).astype(bf16)
        down_s[cols, :] = mm(aT, dlow_s[...]).astype(bf16)
        return carry

    lax.fori_loop(0, FF // CHUNK, hidden_chunk, 0)
    if remote:
        links.scatter_step(UP, 0)
    y_s[...] = y_s[...].T
    layer_out[...] = y_s[:D, :]

    def down_groups(k, carry):
        part = mm(widen[:256, :240], down_s[pl.ds(pl.multiple_of(k * 240, 16), 240), :]).astype(bf16)
        mine = (k // 4, (k // 2) % 2, k % 2)
        for c in range(4):
            where = mine + (slice(None),) * 2 + (slice(DOWN0 + 4 * c, DOWN0 + 4 * c + 4),)
            G[where] = part[:, c * LANES : (c + 1) * LANES].reshape(2, 2, 4, 16, LANES)
        return carry

    lax.fori_loop(0, NDP, down_groups, 0)

    d_from, dg2, db2 = norm_back(dn_s[...], plain2[...], inverse2, gains[2:3])
    d_res = dres_s[...] + d_from
    dres_s[...] = d_res
    dlow_s[...] = d_res.astype(bf16)

    for t in range(NTEN):
        dA_s[t] = mm_nt(dlow_s[...], out_s[t]).astype(bf16)
        dAT = mm_nt(out_s[t], dlow_s[...]).astype(bf16).astype(f32)
        product = OT_s[t] * strided(dAT)
        for j in range(HEADS_DEV):
            centre_s[t, j : j + 1, :] = jnp.sum(product[j * 32 : j * 32 + HEAD], axis=0, keepdims=True)
        attT = mm_nt(widen[:LANES, :LANES], att_s[t]).astype(bf16)
        part = mm(attT, dlow_s[...]).astype(bf16)
        mine = (slice(None),) * 3 + (t // 2, t % 2)
        for c in range(4):
            G[mine + (OUT0 + c,)] = part[:, c * LANES : (c + 1) * LANES].reshape(2, 2, 2, 16, LANES)
    if remote:
        links.scatter_step(DOWN, 0)
        links.scatter_step(UP, 1)

    dk_s[...] = jnp.zeros_like(dk_s)
    dv_s[...] = jnp.zeros_like(dv_s)

    def backward_head(h, carry):
        t = h // HEADS_DEV
        j = h - t * HEADS_DEV
        begin = j * HEAD
        lanes = jnp.where((lane_id >= begin) & (lane_id < begin + HEAD), 1.0, 0.0).astype(bf16)
        rows = pl.ds(pl.multiple_of(j * 32, 32), 32)
        values = v_s[t]
        keysT = kT_s[t, rows, :]
        dA = dA_s[t] * lanes
        for b in range(MAXLEN // QB):
            cols = slice(b * QB, (b + 1) * QB)
            dP = mm_nt(values, dA[cols])
            ds = (P_s[h, :, cols].astype(f32) * (dP - centre_s[t, pl.ds(j, 1), cols])).astype(bf16)
            ds_s[:, cols] = ds
            dqT_s[t, rows, cols] = mm(keysT, ds)
        dv_s[t] += mm(P_s[h], dA)
        dk_s[t] += mm(ds_s[...], q_s[t] * lanes)
        if remote:
            for when, group, number in SCATTER_AT:
                pl.when(h == when)(functools.partial(links.scatter_step, group, number))
        return carry

    lax.fori_loop(0, NTEN * HEADS_DEV, backward_head, 0)

    for t in range(NTEN):
        first_lane = t * 3 * LANES
        for number in range(2):
            g = (dense(dqT_s[t]).T if number == 0 else dk_s[t]) * scale
            r = g * cosv - pltpu.roll(g, LANES - 12, 1) * firstv - pltpu.roll(g, 12, 1) * secondv
            dj_s[:, first_lane + number * LANES : first_lane + (number + 1) * LANES] = r.astype(bf16)
        dj_s[:, first_lane + 2 * LANES : first_lane + 3 * LANES] = dv_s[t].astype(bf16)
    for pair in range(2):
        part = mm(act_pad1[...], dj_s[:, pair * (JOINED // 2) : (pair + 1) * (JOINED // 2)]).astype(bf16)
        for number in range(6):
            t, c = 2 * pair + number // 3, number % 3
            where = (slice(None),) * 3 + (t // 2, t % 2) + (slice(QKV0 + 4 * c, QKV0 + 4 * c + 4),)
            G[where] = part[:, number * LANES : (number + 1) * LANES].reshape(2, 2, 2, 4, 16, LANES)
    if remote:
        links.scatter_step(EARLY, 0)
        links.scatter_step(UP, 5)
        links.scatter_step(DOWN, 5)
    dz = mm_nt(dj_s[...], qkv_s[...])
    d_from, dg1, db1 = norm_back(dz, plain1[...], inverse1, gains[0:1])
    norm_parts = jnp.concatenate([dg1, db1, dg2, db2, jnp.zeros((4, WIDE), f32)], 0)
    if remote:
        links.norm_start(norm_parts)
        links.scatter_step(EARLY, 1)
    else:
        norm_out[...] = norm_parts
    x_s[...] = (dres_s[...] + d_from).T
    tokens_grad[...] = x_s[:D, :]
    if remote:
        links.norm_step(0)
        links.scatter_step(EARLY, 2)
        links.norm_step(1)
        links.scatter_step(EARLY, 3)
        links.norm_step(2)
        links.scatter_step(EARLY, 4)
        links.scatter_step(EARLY, 5)
        links.finish()


def run_layer(lengths, clusters, cluster_weight, source, tokens, cotangent, norm_master, remote):
    rows = MAXLEN
    wide_norm = jnp.pad(norm_master, ((0, 0), (0, WIDE - D)))
    smem = pl.BlockSpec(memory_space=pltpu.SMEM)
    vmem = pl.BlockSpec(memory_space=pltpu.VMEM)
    head_set = (NTEN, MAXLEN, LANES)
    turned = (NTEN, HEADS_DEV * 32, MAXLEN)
    wide = (rows, WIDE)
    scratch = [
        pltpu.VMEM((WIDE, FF), bf16),
        pltpu.VMEM((FF, WIDE), bf16),
        pltpu.VMEM((WIDE, JOINED), bf16),
        pltpu.VMEM((WIDE, JOINED), bf16),
        pltpu.VMEM((NTEN, LANES, WIDE), bf16),
        pltpu.VMEM(head_set, bf16),
        pltpu.VMEM(head_set, bf16),
        pltpu.VMEM(head_set, bf16),
        pltpu.VMEM(turned, bf16),
        pltpu.VMEM(turned, bf16),
        pltpu.VMEM((NTEN * HEADS_DEV, MAXLEN, MAXLEN), bf16),
        pltpu.VMEM(turned, f32),
        pltpu.VMEM(head_set, bf16),
        pltpu.VMEM(head_set, bf16),
        pltpu.VMEM(turned, f32),
        pltpu.VMEM(head_set, f32),
        pltpu.VMEM(head_set, f32),
        pltpu.VMEM(wide, bf16),
        pltpu.VMEM(wide, bf16),
        pltpu.VMEM(wide, bf16),
        pltpu.VMEM(wide, f32),
        pltpu.VMEM(wide, f32),
        pltpu.VMEM(wide, f32),
        pltpu.VMEM(wide, f32),
        pltpu.VMEM(wide, f32),
        pltpu.VMEM(wide, f32),
        pltpu.VMEM(wide, bf16),
        pltpu.VMEM((CHUNK, CHUNK), bf16),
        pltpu.VMEM(wide, f32),
        pltpu.VMEM((NTEN, 8, MAXLEN), f32),
        pltpu.VMEM((MAXLEN, MAXLEN), bf16),
        pltpu.VMEM(wide, bf16),
    ]
    tiles = (TILES, 16, LANES)
    params = dict(vmem_limit_bytes=66_900_000)
    if remote:
        result = jax.ShapeDtypeStruct(tiles, f32)
        scratch += Links.scratch()
        params.update(collective_id=0, has_side_effects=True)
    else:
        result = jax.ShapeDtypeStruct((2,) * 5 + tiles, bf16)
        source = source.reshape((2,) * 5 + tiles)
    turned_out, turned_grad, grads, norm_grad = pl.pallas_call(
        functools.partial(layer_kernel, remote),
        out_shape=(
            jax.ShapeDtypeStruct((D, rows), f32),
            jax.ShapeDtypeStruct((D, rows), f32),
            result,
            jax.ShapeDtypeStruct((8, WIDE), f32),
        ),
        in_specs=[smem] * 3 + [vmem] * 9,
        out_specs=[vmem] * 4,
        scratch_shapes=scratch,
        compiler_params=pltpu.CompilerParams(**params),
        name="layer",
    )(lengths, clusters, cluster_weight, source, tokens.T, cotangent.T, wide_norm, *constants())
    if not remote:
        grads = grads.reshape(NDP, NTEN, *tiles)
    return turned_out.T, turned_grad.T, grads, norm_grad


def shard_tiles(up, down, qkv, out):
    up = jnp.pad(up.reshape(15, 15, LANES), ((0, 1), (0, 0), (0, 0))).transpose(1, 0, 2)
    down = jnp.pad(down.reshape(4, 15, D), ((0, 0), (0, 1), (0, WIDE - D)))
    down = down.reshape(4, 16, 4, LANES).transpose(2, 0, 1, 3).reshape(16, 16, LANES)
    qkv = jnp.pad(qkv.reshape(4, 15, 3, 120), ((0, 0), (0, 1), (0, 0), (0, LANES - 120)))
    qkv = qkv.transpose(2, 0, 1, 3).reshape(12, 16, LANES)
    out = jnp.pad(out.reshape(15, D), ((0, 1), (0, WIDE - D)))
    out = out.reshape(16, 4, LANES).transpose(1, 0, 2)
    return jnp.concatenate([up, out, down, qkv], 0)


def tiles_shard(tiles):
    up = tiles[UP0:OUT0, :15].transpose(1, 0, 2).reshape(-1)
    down = tiles[DOWN0:QKV0].reshape(4, 4, 16, LANES).transpose(1, 2, 0, 3)[:, :15].reshape(60, WIDE)[:, :D].reshape(-1)
    qkv = tiles[QKV0:].reshape(3, 4, 16, LANES).transpose(1, 2, 0, 3)[:, :15, :, :120].reshape(1, -1)
    out = tiles[OUT0:DOWN0].transpose(1, 0, 2)[:15].reshape(15, WIDE)[:, :D].reshape(1, -1)
    return up, down, qkv, out


def adam_step(master, moment, square, average, grad, rate):
    moment_new = beta_one * moment + (1.0 - beta_one) * grad
    square_new = beta_two * square + (1.0 - beta_two) * grad * grad
    update = moment_new / (jnp.sqrt(square_new) + adam_eps) + decay_rate * master
    fresh = master - rate * update
    average_new = average_keep * average + (1.0 - average_keep) * fresh
    return (fresh, moment_new, square_new, average_new)


def to_groups(up, down, qkv, out):
    up, down = up.reshape(NDP, NTEN, -1), down.reshape(NDP, NTEN, -1)
    qkv = qkv.reshape(NTEN, NDP, -1).transpose(1, 0, 2)
    out = out.reshape(NTEN, NDP, -1).transpose(1, 0, 2)
    return jax.vmap(jax.vmap(shard_tiles))(up, down, qkv, out)


def from_groups(tiles):
    up, down, qkv, out = jax.vmap(jax.vmap(tiles_shard))(tiles.astype(f32))
    qkv = qkv.reshape(NDP, NTEN, -1).transpose(1, 0, 2).reshape(NTEN, -1)
    out = out.reshape(NDP, NTEN, -1).transpose(1, 0, 2).reshape(NTEN, -1)
    return up.reshape(-1), down.reshape(-1), qkv, out


def on_device(tokens, cotangent, lengths, clusters, cluster_weight, *state):
    qkv, out, up, down, norm = (state[4 * k : 4 * k + 4] for k in range(5))
    ends = ("dp", "tensor")
    low = tuple(w[0].astype(bf16) for w in (up, down, qkv, out))
    grid = (lax.axis_size("dp"), lax.axis_size("tensor")) == (NDP, NTEN)
    if grid:
        source = shard_tiles(*low)
    else:
        whole = [lax.all_gather(w, ends, axis=0, tiled=True) for w in low[:2]]
        for w in low[2:]:
            block = lax.all_gather(w, "dp", axis=1, tiled=True)
            whole.append(lax.all_gather(block, "tensor", axis=0, tiled=True))
        source = to_groups(*whole)
    layer_out, tokens_grad, total, norm_total = run_layer(
        lengths, clusters, cluster_weight, source, tokens, cotangent, norm[0], grid
    )
    if grid:
        grads = tiles_shard(total)
    else:
        whole = from_groups(total)
        grads = [lax.psum_scatter(g, ends, scatter_dimension=0, tiled=True) for g in whole[:2]]
        for g in whole[2:]:
            block = lax.psum_scatter(g, "tensor", scatter_dimension=0, tiled=True)
            grads.append(lax.psum_scatter(block, "dp", scatter_dimension=1, tiled=True))
        norm_total = lax.psum(norm_total, ends)
    up_grad, down_grad, qkv_grad, out_grad = grads
    results = (layer_out, tokens_grad)
    results += adam_step(*qkv, qkv_grad, D ** (-0.5))
    results += adam_step(*out, out_grad, (D // 32) ** (-0.5))
    results += adam_step(*up, up_grad, D ** (-0.5))
    results += adam_step(*down, down_grad, FF ** (-0.5))
    results += adam_step(*norm, norm_total[:4, :D], 0.2)
    return results


def solution(mesh):
    rows, both, flat = P(("dp", "tensor"), None), P("tensor", "dp"), P(("dp", "tensor"))
    state = (both,) * 8 + (flat,) * 8 + (P(),) * 4
    return jax.shard_map(
        on_device,
        mesh=mesh,
        in_specs=(rows, rows, P("dp"), P("dp"), P()) + state,
        out_specs=(rows, rows) + state,
        check_vma=False,
    )
```

```python
import functools

import jax
import jax.numpy as jnp
import numpy as np
from jax import lax
from jax.experimental import pallas as pl
from jax.experimental.pallas import tpu as pltpu
from jax.sharding import PartitionSpec as P

D = 480
HEAD = 24
FF = 1920
MAXLEN = 512
NDP, NTEN = 8, 4
WIDE = 512
HEADS_DEV = 5
LANES = 128
TILES = 47
JOINED = 1536
UP0, OUT0, DOWN0, QKV0 = 0, 15, 19, 35
CHUNK = 384
QB = 512
SPARE = 120

norm_eps = 1e-05
beta_one = 0.5
beta_two = 0.5
adam_eps = 1e-08
decay_rate = 0.01
average_keep = 0.75
hidden_score = -1e38
MESH = pl.DeviceIdType.MESH
f32, bf16 = jnp.float32, jnp.bfloat16


def mm(a, b):
    return lax.dot_general(a, b, (((1,), (0,)), ((), ())), preferred_element_type=f32)


def mm_nt(a, b):
    return lax.dot_general(a, b, (((1,), (1,)), ((), ())), preferred_element_type=f32)


def constants():
    natural = np.arange(D)
    squeeze = np.zeros((WIDE, WIDE), np.float32)
    squeeze[natural, 16 * (natural // 15) + natural % 15] = 1.0
    position = np.arange(MAXLEN, dtype=np.float32)
    exponent = np.arange(HEAD // 2, dtype=np.float32) * np.float32(2.0 / HEAD)
    inverse = np.float32(10000.0) ** (-exponent)
    angle = (position[:, None] * inverse[None, :]).astype(np.float32).astype(np.float64)
    lane = np.arange(120)
    place = lane % HEAD
    cosine = np.zeros((MAXLEN, LANES), np.float32)
    first = np.zeros((MAXLEN, LANES), np.float32)
    second = np.zeros((MAXLEN, LANES), np.float32)
    cosine[:, :120] = np.cos(angle)[:, place % 12]
    sines = np.sin(angle)[:, place % 12]
    first[:, :120] = np.where(place < 12, -sines, 0.0)
    second[:, :120] = np.where(place >= 12, sines, 0.0)
    low = lambda v: jnp.asarray(v.astype(jnp.bfloat16))
    return (low(squeeze), low(squeeze.T), jnp.asarray(cosine), jnp.asarray(first), jnp.asarray(second))


UP, DOWN, EARLY, OUT = (0, 1, 2), (3, 4, 5), (6, 7, 8), (9, 10)
WAY_A, WAY_B, WAY_C = (0, 1, 3, 2, 4), (0, 1, 2, 3, 4), (2, 3, 0, 1, 4)
GATHER_ROUTES = (
    (0, 8, WAY_A), (8, 8, WAY_B), (16, 3, WAY_C),
    (19, 6, WAY_A), (25, 7, WAY_B), (32, 3, WAY_C),
    (35, 5, WAY_A), (40, 5, WAY_B), (45, 2, WAY_C),
)
SCATTER_ROUTES = (
    (0, 6, WAY_A), (6, 6, WAY_B), (12, 3, WAY_C),
    (19, 6, WAY_A), (25, 7, WAY_B), (32, 3, WAY_C),
    (35, 5, WAY_A), (40, 5, WAY_B), (45, 2, WAY_C),
    (15, 2, WAY_A), (17, 2, WAY_B),
)
GATHER_AT = ((1, DOWN, 1), (3, UP, 3), (5, DOWN, 2), (10, UP, 4), (11, DOWN, 3), (18, DOWN, 4))
SCATTER_AT = ((2, OUT, 1), (5, UP, 2), (11, DOWN, 2), (13, OUT, 2), (14, UP, 3), (16, DOWN, 3), (17, OUT, 3), (18, UP, 4))


class Links:
    @staticmethod
    def scratch():
        n, tiles = len(SCATTER_ROUTES), (TILES, 16, LANES)
        bufs = [
            pltpu.VMEM((2,) * (4 - stage) + (count, 16, LANES), bf16)
            for begin, count, order in SCATTER_ROUTES
            for stage in range(5)
        ]
        return bufs + [
            pltpu.VMEM((2,) * 5 + tiles, bf16),
            pltpu.VMEM((2,) * 5 + tiles, bf16),
            pltpu.VMEM((3, 8, WIDE), f32),
            pltpu.VMEM((3, 4, 8, WIDE), f32),
            pltpu.SemaphoreType.DMA,
            pltpu.SemaphoreType.DMA((n, 5)),
            pltpu.SemaphoreType.DMA((n, 5)),
            pltpu.SemaphoreType.DMA((n, 5)),
            pltpu.SemaphoreType.DMA((n, 5)),
            pltpu.SemaphoreType.DMA((3, 3)),
            pltpu.SemaphoreType.DMA((3, 3)),
        ]

    def __init__(self, shard, total, norm_total, *scratch):
        n = len(SCATTER_ROUTES)
        self.shard, self.total, self.norm_total = shard, total, norm_total
        self.bufs = [scratch[5 * r : 5 * r + 5] for r in range(n)]
        (
            self.whole, self.parts, self.norm_now, self.norm_in, self.own_sem,
            self.g_send, self.g_recv, self.s_send, self.s_recv, self.n_send, self.n_recv,
        ) = scratch[5 * n :]
        dp, tensor = lax.axis_index("dp"), lax.axis_index("tensor")
        self.coords = (dp // 4, (dp // 2) % 2, dp % 2, tensor // 2, tensor % 2)

    def partner(self, dim):
        c = list(self.coords)
        c[dim] = 1 - c[dim]
        return (c[0] * 4 + c[1] * 2 + c[2], c[3] * 2 + c[4])

    def peers(self, group):
        z0, z1, x, y, core = self.coords
        found = []
        if group == 0:
            mine = z0 * 2 + z1
            for step in range(1, 4):
                z = (mine + step) % 4
                found.append(((z * 2 + x, y * 2 + core), z))
        elif group == 1:
            mine = x * 2 + y
            for dx, dy in ((0, 1), (1, 0), (1, 1)):
                px, py = (x + dx) % 2, (y + dy) % 2
                found.append((((z0 * 2 + z1) * 2 + px, py * 2 + core), px * 2 + py))
        else:
            mine = core
            found.append((((z0 * 2 + z1) * 2 + x, y * 2 + 1 - core), 1 - core))
        return found, mine

    def greet(self):
        barrier = pltpu.get_barrier_semaphore()
        others = [device for group in range(3) for device, slot in self.peers(group)[0]]
        for device in others:
            pl.semaphore_signal(barrier, inc=1, device_id=device, device_id_type=MESH)
        pl.semaphore_wait(barrier, len(others))

    def keep_own(self):
        copy = pltpu.make_async_copy(self.shard, self.whole.at[self.coords], self.own_sem)
        copy.start()
        copy.wait()

    def gather_copy(self, r, stage):
        begin, count, order = GATHER_ROUTES[r]
        done, dim = order[:stage], order[stage]
        where = tuple(slice(None) if d in done else self.coords[d] for d in range(5)) + (pl.ds(begin, count),)
        return pltpu.make_async_remote_copy(
            src_ref=self.whole.at[where],
            dst_ref=self.whole.at[where],
            send_sem=self.g_send.at[r, stage],
            recv_sem=self.g_recv.at[r, stage],
            device_id=self.partner(dim),
            device_id_type=MESH,
        )

    def gather_step(self, group, stage):
        for r in group:
            if stage > 0:
                self.gather_copy(r, stage - 1).wait_recv()
            if stage < 5:
                self.gather_copy(r, stage).start()

    def sums(self, r, stage, coordinate):
        begin, count, order = SCATTER_ROUTES[r]
        order = order[::-1]
        left = [d for d in range(5) if d not in order[:stage]]
        where = tuple(coordinate if d == order[stage] else slice(None) for d in left)
        if stage == 0:
            return self.parts.at[where + (pl.ds(begin, count),)]
        return self.bufs[r][stage - 1].at[where]

    def scatter_copy(self, r, stage):
        dim = SCATTER_ROUTES[r][2][4 - stage]
        return pltpu.make_async_remote_copy(
            src_ref=self.sums(r, stage, 1 - self.coords[dim]),
            dst_ref=self.bufs[r][stage],
            send_sem=self.s_send.at[r, stage],
            recv_sem=self.s_recv.at[r, stage],
            device_id=self.partner(dim),
            device_id_type=MESH,
        )

    def scatter_step(self, group, stage):
        for r in group:
            begin, count, order = SCATTER_ROUTES[r]
            if stage > 0:
                self.scatter_copy(r, stage - 1).wait_recv()
                buf = self.bufs[r][stage - 1]
                mine = self.sums(r, stage - 1, self.coords[order[5 - stage]])[...]
                if stage < 5:
                    buf[...] = buf[...] + mine
                else:
                    self.total[begin : begin + count] = buf[...].astype(f32) + mine.astype(f32)
            if stage < 5:
                self.scatter_copy(r, stage).start()

    def norm_copies(self, group):
        found, mine = self.peers(group)
        return [
            pltpu.make_async_remote_copy(
                src_ref=self.norm_now.at[group],
                dst_ref=self.norm_in.at[group, mine],
                send_sem=self.n_send.at[group, k],
                recv_sem=self.n_recv.at[group, k],
                device_id=device,
                device_id_type=MESH,
            )
            for k, (device, slot) in enumerate(found)
        ]

    def norm_start(self, values, group=0):
        self.norm_now[group] = values
        self.norm_in[group, self.peers(group)[1]] = values
        for copy in self.norm_copies(group):
            copy.start()

    def norm_step(self, group):
        for copy in self.norm_copies(group):
            copy.wait_recv()
        now = self.norm_in[group, 0]
        for slot in range(1, 2 if group == 2 else 4):
            now = now + self.norm_in[group, slot]
        if group < 2:
            self.norm_start(now, group + 1)
        else:
            self.norm_total[...] = now

    def finish(self):
        for stage in range(5):
            for r in range(len(GATHER_ROUTES)):
                self.gather_copy(r, stage).wait_send()
            for r in range(len(SCATTER_ROUTES)):
                self.scatter_copy(r, stage).wait_send()
        for group in range(3):
            for copy in self.norm_copies(group):
                copy.wait_send()


def gelu_parts(u):
    half = 0.5 * (1.0 + lax.erf(u * 0.7071067811865476))
    return u * half, half + u * jnp.exp(-0.5 * u * u) * 0.3989422804014327


def layer_kernel(remote, *refs):
    lengths, clusters, weights_of, source, tok, cot, norm, squeeze, widen, cosine, first, second = refs[:12]
    layer_out, tokens_grad, G_out, norm_out = refs[12:16]
    (
        up_s, down_s, qkv_s, dj_s, out_s, q_s, k_s, v_s, kT_s, vT_s, P_s, OT_s, att_s, dA_s, dqT_s, dk_s, dv_s,
        act1_s, act2_s, act_pad, plain1, plain2, res_s, y_s, dn_s, dres_s, dlow_s, eye_s, x_s, centre_s, ds_s, act_pad1, norm_s, rows_s, read_sem,
    ) = refs[16:51]
    if remote:
        links = Links(source, G_out, norm_out, *refs[51:])
        W, G = links.whole, links.parts
        links.greet()
        links.keep_own()
        links.gather_step(EARLY, 0)
    else:
        links, W, G = None, source, G_out
    me = lax.axis_index("tensor")
    length = lengths[me]
    scale_row = weights_of[clusters[me]]
    scale = HEAD ** -0.5

    lane = lax.broadcasted_iota(jnp.int32, (1, WIDE), 1)
    real = jnp.where(lane < D, 1.0, 0.0)
    norm_s[...] = jnp.zeros_like(norm_s)
    norm_s[:4, :D] = norm[...]
    gains = norm_s[...]

    def norm_rows(values, gain, shift):
        middle = jnp.sum(values, axis=-1, keepdims=True) * (1.0 / D)
        centered = (values - middle) * real
        spread_ = jnp.sum(centered * centered, axis=-1, keepdims=True) * (1.0 / D)
        inverse = lax.rsqrt(spread_ + norm_eps)
        plain = centered * inverse
        return plain * gain + shift, plain, inverse

    def norm_back(dz, plain, inverse, gain):
        dg = jnp.sum(dz * plain, axis=0, keepdims=True)
        db = jnp.sum(dz, axis=0, keepdims=True)
        scaled = dz * gain
        one = jnp.sum(scaled, axis=-1, keepdims=True) * (1.0 / D)
        two = jnp.sum(scaled * plain, axis=-1, keepdims=True) * (1.0 / D)
        return inverse * (scaled - one - plain * two) * real, dg, db

    reads = [pltpu.make_async_copy(ref, rows_s.at[k], read_sem.at[k]) for k, ref in enumerate((tok, cot))]
    for read in reads:
        read.start()
    x_s[...] = jnp.zeros_like(x_s)
    dres_s[...] = jnp.zeros_like(dres_s)
    for read in reads:
        read.wait()
    x_s[:D, :] = rows_s[0].astype(f32)
    dres_s[:D, :] = rows_s[1].astype(f32)
    x_s[...] = x_s[...].T
    normed, plain, inverse1 = norm_rows(x_s[...], gains[0:1], gains[1:2])
    plain1[...] = plain
    act1_s[...] = normed.astype(bf16)
    if remote:
        links.gather_step(EARLY, 1)
    row = lax.broadcasted_iota(jnp.int32, (MAXLEN, 1), 0)
    row_scale = jnp.where(row < length, scale_row, 0.0)
    dres_s[...] = dres_s[...].T * row_scale
    dlow_s[...] = dres_s[...].astype(bf16)
    act_pad1[...] = mm_nt(widen[...], act1_s[...]).astype(bf16)
    if remote:
        links.gather_step(EARLY, 2)
        links.gather_step(UP, 0)
        links.gather_step(EARLY, 3)
        links.gather_step(EARLY, 4)
        links.gather_step(UP, 1)
        links.gather_step(EARLY, 5)
        links.gather_step(UP, 2)
        links.gather_step(DOWN, 0)

    for pair in range(2):
        pieces = []
        for t in (2 * pair, 2 * pair + 1):
            mine = (slice(None),) * 3 + (t // 2, t % 2)
            pieces += [W[mine + (slice(QKV0 + 4 * c, QKV0 + 4 * c + 4),)].reshape(WIDE, LANES) for c in range(3)]
        half = slice(pair * (JOINED // 2), (pair + 1) * (JOINED // 2))
        qkv_s[:, half] = mm(squeeze[...], jnp.concatenate(pieces, 1)).astype(bf16)
    cosv, firstv, secondv = cosine[...], first[...], second[...]
    lane_id = lax.broadcasted_iota(jnp.int32, (1, LANES), 1)
    key_id = lax.broadcasted_iota(jnp.int32, (MAXLEN, 1), 0)
    spare = jnp.where(lane_id == SPARE, 1.0, 0.0)
    key_bias = jnp.where(key_id < length, 0.0, hidden_score) * spare

    def strided(block):
        gap = jnp.zeros((8, MAXLEN), f32)
        return jnp.concatenate([x for j in range(HEADS_DEV) for x in (block[j * HEAD : (j + 1) * HEAD], gap)], 0)

    def dense(block):
        rows = [block[j * 32 : j * 32 + HEAD] for j in range(HEADS_DEV)]
        return jnp.concatenate(rows + [jnp.zeros((8, MAXLEN), f32)], 0)

    for t in range(NTEN):
        if t % 2 == 0:
            both = mm(act1_s[...], qkv_s[:, t * 3 * LANES : (t + 2) * 3 * LANES])
        joined = both[:, (t % 2) * 3 * LANES : (t % 2 + 1) * 3 * LANES]
        for number in range(2):
            u = joined[:, number * LANES : (number + 1) * LANES]
            r = u * cosv + pltpu.roll(u, LANES - 12, 1) * firstv + pltpu.roll(u, 12, 1) * secondv
            if number == 0:
                q_s[t] = (r + spare).astype(bf16)
            else:
                k_s[t] = (r + key_bias).astype(bf16)
                kT_s[t] = strided(r.T).astype(bf16)
        v = joined[:, 2 * LANES :]
        v_s[t] = v.astype(bf16)
        vT_s[t] = strided(v.T).astype(bf16)

    fold = HEAD ** -0.5 * 1.4426950408889634

    def forward_head(h, carry):
        t = h // HEADS_DEV
        j = h - t * HEADS_DEV
        begin = j * HEAD
        kept = ((lane_id >= begin) & (lane_id < begin + HEAD)) | (lane_id == SPARE)
        keys = k_s[t] * jnp.where(kept, 1.0, 0.0).astype(bf16)
        rows = pl.ds(pl.multiple_of(j * 32, 32), 32)
        values = vT_s[t, rows, :]
        for b in range(MAXLEN // QB):
            cols = slice(b * QB, (b + 1) * QB)
            s = mm_nt(keys, q_s[t, cols, :])
            top = jnp.max(s, axis=0, keepdims=True)
            e = jnp.exp2(s * fold - top * fold)
            total = jnp.sum(e, axis=0, keepdims=True)
            p = (e * (1.0 / total)).astype(bf16)
            P_s[h, :, cols] = p
            OT_s[t, rows, cols] = mm(values, p)
        if remote:
            for when, group, number in GATHER_AT:
                pl.when(h == when)(functools.partial(links.gather_step, group, number))
        return carry

    lax.fori_loop(0, NTEN * HEADS_DEV, forward_head, 0)

    if remote:
        links.gather_step(UP, 5)
    res = x_s[...]
    for t in range(NTEN):
        mine = (slice(None),) * 3 + (t // 2, t % 2)
        pieces = [W[mine + (OUT0 + c,)].reshape(LANES, LANES) for c in range(4)]
        out_s[t] = mm(squeeze[:LANES, :LANES], jnp.concatenate(pieces, 1)).astype(bf16)
        att_s[t] = dense(OT_s[t]).T.astype(bf16)
        res = res + mm(att_s[t], out_s[t])
    res_s[...] = res
    normed, plain, inverse2 = norm_rows(res, gains[2:3], gains[3:4])
    plain2[...] = plain
    act2_s[...] = normed.astype(bf16)
    act_pad[...] = mm_nt(widen[...], act2_s[...]).astype(bf16)

    for c in range(8):
        pieces = [W[:, :, :, :, :, UP0 + n].reshape(WIDE, LANES) for n in range(2 * c, min(2 * c + 2, 15))]
        up_s[:, 2 * c * LANES : (2 * c + len(pieces)) * LANES] = mm(squeeze[...], jnp.concatenate(pieces, 1)).astype(bf16)

    if remote:
        links.gather_step(DOWN, 5)

    def down_rows(k, carry):
        mine = (k // 4, (k // 2) % 2, k % 2)
        pieces = [W[mine + (slice(None),) * 2 + (slice(DOWN0 + 4 * c, DOWN0 + 4 * c + 4),)].reshape(256, LANES) for c in range(4)]
        part = mm(squeeze[:240, :256], jnp.concatenate(pieces, 1)).astype(bf16)
        down_s[pl.ds(pl.multiple_of(k * 240, 16), 240), :] = part
        return carry

    lax.fori_loop(0, NDP, down_rows, 0)

    y_s[...] = res_s[...]
    dn_s[...] = jnp.zeros_like(dn_s)
    eye_row = lax.broadcasted_iota(jnp.int32, (CHUNK, CHUNK), 0)
    eye_col = lax.broadcasted_iota(jnp.int32, (CHUNK, CHUNK), 1)
    eye = jnp.where(eye_row == eye_col, 1.0, 0.0).astype(bf16)
    eye_s[...] = eye

    def hidden_chunk(c, carry):
        cols = pl.ds(pl.multiple_of(c * CHUNK, LANES), CHUNK)
        u = mm(act2_s[...], up_s[:, cols])
        value, slope = gelu_parts(u)
        a = value.astype(bf16)
        y_s[...] += mm(a, down_s[cols, :])
        d_active = mm_nt(dlow_s[...], down_s[cols, :])
        d_upper = (d_active * slope).astype(bf16)
        dn_s[...] += mm_nt(d_upper, up_s[:, cols])
        g_up = mm(act_pad[...], d_upper).astype(bf16)
        for part in range(3):
            G[:, :, :, :, :, UP0 + 3 * c + part] = g_up[:, part * LANES : (part + 1) * LANES].reshape(2, 2, 2, 2, 2, 16, LANES)
        aT = mm_nt(eye_s[...], a).astype(bf16)
        down_s[cols, :] = mm(aT, dlow_s[...]).astype(bf16)
        return carry

    lax.fori_loop(0, FF // CHUNK, hidden_chunk, 0)
    if remote:
        links.scatter_step(UP, 0)
    y_s[...] = y_s[...].T
    layer_out[...] = y_s[:D, :]

    def down_groups(k, carry):
        part = mm(widen[:256, :240], down_s[pl.ds(pl.multiple_of(k * 240, 16), 240), :]).astype(bf16)
        mine = (k // 4, (k // 2) % 2, k % 2)
        for c in range(4):
            where = mine + (slice(None),) * 2 + (slice(DOWN0 + 4 * c, DOWN0 + 4 * c + 4),)
            G[where] = part[:, c * LANES : (c + 1) * LANES].reshape(2, 2, 4, 16, LANES)
        return carry

    lax.fori_loop(0, NDP, down_groups, 0)
    if remote:
        links.scatter_step(DOWN, 0)

    d_from, dg2, db2 = norm_back(dn_s[...], plain2[...], inverse2, gains[2:3])
    d_res = dres_s[...] + d_from
    dres_s[...] = d_res
    dlow_s[...] = d_res.astype(bf16)

    if remote:
        links.scatter_step(UP, 1)
    for t in range(NTEN):
        dA_s[t] = mm_nt(dlow_s[...], out_s[t]).astype(bf16)
        dAT = mm_nt(out_s[t], dlow_s[...]).astype(bf16).astype(f32)
        product = OT_s[t] * strided(dAT)
        for j in range(HEADS_DEV):
            centre_s[t, j : j + 1, :] = jnp.sum(product[j * 32 : j * 32 + HEAD], axis=0, keepdims=True)
        attT = mm_nt(widen[:LANES, :LANES], att_s[t]).astype(bf16)
        part = mm(attT, dlow_s[...]).astype(bf16)
        mine = (slice(None),) * 3 + (t // 2, t % 2)
        for c in range(4):
            G[mine + (OUT0 + c,)] = part[:, c * LANES : (c + 1) * LANES].reshape(2, 2, 2, 16, LANES)
    if remote:
        links.scatter_step(OUT, 0)
        links.scatter_step(DOWN, 1)

    dk_s[...] = jnp.zeros_like(dk_s)
    dv_s[...] = jnp.zeros_like(dv_s)

    def backward_head(h, carry):
        t = h // HEADS_DEV
        j = h - t * HEADS_DEV
        begin = j * HEAD
        lanes = jnp.where((lane_id >= begin) & (lane_id < begin + HEAD), 1.0, 0.0).astype(bf16)
        rows = pl.ds(pl.multiple_of(j * 32, 32), 32)
        values = v_s[t]
        keysT = kT_s[t, rows, :]
        dA = dA_s[t] * lanes
        for b in range(MAXLEN // QB):
            cols = slice(b * QB, (b + 1) * QB)
            dP = mm_nt(values, dA[cols])
            ds = (P_s[h, :, cols].astype(f32) * (dP - centre_s[t, pl.ds(j, 1), cols])).astype(bf16)
            ds_s[:, cols] = ds
            dqT_s[t, rows, cols] = mm(keysT, ds)
        dv_s[t] += mm(P_s[h], dA)
        dk_s[t] += mm(ds_s[...], q_s[t] * lanes)
        if remote:
            for when, group, number in SCATTER_AT:
                pl.when(h == when)(functools.partial(links.scatter_step, group, number))
        return carry

    lax.fori_loop(0, NTEN * HEADS_DEV, backward_head, 0)

    for t in range(NTEN):
        first_lane = t * 3 * LANES
        for number in range(2):
            g = (dense(dqT_s[t]).T if number == 0 else dk_s[t]) * scale
            r = g * cosv - pltpu.roll(g, LANES - 12, 1) * firstv - pltpu.roll(g, 12, 1) * secondv
            dj_s[:, first_lane + number * LANES : first_lane + (number + 1) * LANES] = r.astype(bf16)
        dj_s[:, first_lane + 2 * LANES : first_lane + 3 * LANES] = dv_s[t].astype(bf16)
    for pair in range(2):
        part = mm(act_pad1[...], dj_s[:, pair * (JOINED // 2) : (pair + 1) * (JOINED // 2)]).astype(bf16)
        for number in range(6):
            t, c = 2 * pair + number // 3, number % 3
            where = (slice(None),) * 3 + (t // 2, t % 2) + (slice(QKV0 + 4 * c, QKV0 + 4 * c + 4),)
            G[where] = part[:, number * LANES : (number + 1) * LANES].reshape(2, 2, 2, 4, 16, LANES)
    if remote:
        links.scatter_step(EARLY, 0)
        links.scatter_step(UP, 5)
        links.scatter_step(DOWN, 4)
        links.scatter_step(OUT, 4)
    dz = mm_nt(dj_s[...], qkv_s[...])
    d_from, dg1, db1 = norm_back(dz, plain1[...], inverse1, gains[0:1])
    norm_parts = jnp.concatenate([dg1, db1, dg2, db2, jnp.zeros((4, WIDE), f32)], 0)
    if remote:
        links.norm_start(norm_parts)
        links.scatter_step(EARLY, 1)
    else:
        norm_out[...] = norm_parts
    x_s[...] = (dres_s[...] + d_from).T
    tokens_grad[...] = x_s[:D, :]
    if remote:
        links.norm_step(0)
        links.scatter_step(DOWN, 5)
        links.scatter_step(OUT, 5)
        links.scatter_step(EARLY, 2)
        links.norm_step(1)
        links.scatter_step(EARLY, 3)
        links.norm_step(2)
        links.scatter_step(EARLY, 4)
        links.scatter_step(EARLY, 5)
        links.finish()


def run_layer(lengths, clusters, cluster_weight, source, tokens, cotangent, norm_master, remote):
    rows = MAXLEN
    smem = pl.BlockSpec(memory_space=pltpu.SMEM)
    vmem = pl.BlockSpec(memory_space=pltpu.VMEM)
    hbm = pl.BlockSpec(memory_space=pl.ANY)
    head_set = (NTEN, MAXLEN, LANES)
    turned = (NTEN, HEADS_DEV * 32, MAXLEN)
    wide = (rows, WIDE)
    scratch = [
        pltpu.VMEM((WIDE, FF), bf16),
        pltpu.VMEM((FF, WIDE), bf16),
        pltpu.VMEM((WIDE, JOINED), bf16),
        pltpu.VMEM((WIDE, JOINED), bf16),
        pltpu.VMEM((NTEN, LANES, WIDE), bf16),
        pltpu.VMEM(head_set, bf16),
        pltpu.VMEM(head_set, bf16),
        pltpu.VMEM(head_set, bf16),
        pltpu.VMEM(turned, bf16),
        pltpu.VMEM(turned, bf16),
        pltpu.VMEM((NTEN * HEADS_DEV, MAXLEN, MAXLEN), bf16),
        pltpu.VMEM(turned, f32),
        pltpu.VMEM(head_set, bf16),
        pltpu.VMEM(head_set, bf16),
        pltpu.VMEM(turned, f32),
        pltpu.VMEM(head_set, f32),
        pltpu.VMEM(head_set, f32),
        pltpu.VMEM(wide, bf16),
        pltpu.VMEM(wide, bf16),
        pltpu.VMEM(wide, bf16),
        pltpu.VMEM(wide, f32),
        pltpu.VMEM(wide, f32),
        pltpu.VMEM(wide, f32),
        pltpu.VMEM(wide, f32),
        pltpu.VMEM(wide, f32),
        pltpu.VMEM(wide, f32),
        pltpu.VMEM(wide, bf16),
        pltpu.VMEM((CHUNK, CHUNK), bf16),
        pltpu.VMEM(wide, f32),
        pltpu.VMEM((NTEN, 8, MAXLEN), f32),
        pltpu.VMEM((MAXLEN, MAXLEN), bf16),
        pltpu.VMEM(wide, bf16),
        pltpu.VMEM((8, WIDE), f32),
        pltpu.VMEM((2, D, MAXLEN), bf16),
        pltpu.SemaphoreType.DMA((2,)),
    ]
    tiles = (TILES, 16, LANES)
    params = dict(vmem_limit_bytes=66_900_000)
    if remote:
        result = jax.ShapeDtypeStruct(tiles, f32)
        scratch += Links.scratch()
        params.update(collective_id=0, has_side_effects=True)
    else:
        result = jax.ShapeDtypeStruct((2,) * 5 + tiles, bf16)
        source = source.reshape((2,) * 5 + tiles)
    turned_out, turned_grad, grads, norm_grad = pl.pallas_call(
        functools.partial(layer_kernel, remote),
        out_shape=(
            jax.ShapeDtypeStruct((D, rows), f32),
            jax.ShapeDtypeStruct((D, rows), f32),
            result,
            jax.ShapeDtypeStruct((8, WIDE), f32),
        ),
        in_specs=[smem] * 3 + [vmem, hbm, hbm] + [vmem] * 6,
        out_specs=[vmem] * 4,
        scratch_shapes=scratch,
        compiler_params=pltpu.CompilerParams(**params),
        name="layer",
    )(lengths, clusters, cluster_weight, source, tokens.T, cotangent.T, norm_master, *constants())
    if not remote:
        grads = grads.reshape(NDP, NTEN, *tiles)
    return turned_out.T, turned_grad.T, grads, norm_grad


def shard_tiles(up, down, qkv, out):
    up = jnp.pad(up.reshape(15, 15, LANES), ((0, 1), (0, 0), (0, 0))).transpose(1, 0, 2)
    down = jnp.pad(down.reshape(4, 15, D), ((0, 0), (0, 1), (0, WIDE - D)))
    down = down.reshape(4, 16, 4, LANES).transpose(2, 0, 1, 3).reshape(16, 16, LANES)
    qkv = jnp.pad(qkv.reshape(4, 15, 3, 120), ((0, 0), (0, 1), (0, 0), (0, LANES - 120)))
    qkv = qkv.transpose(2, 0, 1, 3).reshape(12, 16, LANES)
    out = jnp.pad(out.reshape(15, D), ((0, 1), (0, WIDE - D)))
    out = out.reshape(16, 4, LANES).transpose(1, 0, 2)
    return jnp.concatenate([up, out, down, qkv], 0)


def tiles_shard(tiles):
    up = tiles[UP0:OUT0, :15].transpose(1, 0, 2).reshape(-1)
    down = tiles[DOWN0:QKV0].reshape(4, 4, 16, LANES).transpose(1, 2, 0, 3)[:, :15].reshape(60, WIDE)[:, :D].reshape(-1)
    qkv = tiles[QKV0:].reshape(3, 4, 16, LANES).transpose(1, 2, 0, 3)[:, :15, :, :120].reshape(1, -1)
    out = tiles[OUT0:DOWN0].transpose(1, 0, 2)[:15].reshape(15, WIDE)[:, :D].reshape(1, -1)
    return up, down, qkv, out


def adam_step(master, moment, square, average, grad, rate):
    moment_new = beta_one * moment + (1.0 - beta_one) * grad
    square_new = beta_two * square + (1.0 - beta_two) * grad * grad
    update = moment_new / (jnp.sqrt(square_new) + adam_eps) + decay_rate * master
    fresh = master - rate * update
    average_new = average_keep * average + (1.0 - average_keep) * fresh
    return (fresh, moment_new, square_new, average_new)


def to_groups(up, down, qkv, out):
    up, down = up.reshape(NDP, NTEN, -1), down.reshape(NDP, NTEN, -1)
    qkv = qkv.reshape(NTEN, NDP, -1).transpose(1, 0, 2)
    out = out.reshape(NTEN, NDP, -1).transpose(1, 0, 2)
    return jax.vmap(jax.vmap(shard_tiles))(up, down, qkv, out)


def from_groups(tiles):
    up, down, qkv, out = jax.vmap(jax.vmap(tiles_shard))(tiles.astype(f32))
    qkv = qkv.reshape(NDP, NTEN, -1).transpose(1, 0, 2).reshape(NTEN, -1)
    out = out.reshape(NDP, NTEN, -1).transpose(1, 0, 2).reshape(NTEN, -1)
    return up.reshape(-1), down.reshape(-1), qkv, out


def on_device(tokens, cotangent, lengths, clusters, cluster_weight, *state):
    qkv, out, up, down, norm = (state[4 * k : 4 * k + 4] for k in range(5))
    ends = ("dp", "tensor")
    low = tuple(w[0].astype(bf16) for w in (up, down, qkv, out))
    grid = (lax.axis_size("dp"), lax.axis_size("tensor")) == (NDP, NTEN)
    if grid:
        source = shard_tiles(*low)
    else:
        whole = [lax.all_gather(w, ends, axis=0, tiled=True) for w in low[:2]]
        for w in low[2:]:
            block = lax.all_gather(w, "dp", axis=1, tiled=True)
            whole.append(lax.all_gather(block, "tensor", axis=0, tiled=True))
        source = to_groups(*whole)
    layer_out, tokens_grad, total, norm_total = run_layer(
        lengths, clusters, cluster_weight, source, tokens, cotangent, norm[0], grid
    )
    if grid:
        grads = tiles_shard(total)
    else:
        whole = from_groups(total)
        grads = [lax.psum_scatter(g, ends, scatter_dimension=0, tiled=True) for g in whole[:2]]
        for g in whole[2:]:
            block = lax.psum_scatter(g, "tensor", scatter_dimension=0, tiled=True)
            grads.append(lax.psum_scatter(block, "dp", scatter_dimension=1, tiled=True))
        norm_total = lax.psum(norm_total, ends)
    up_grad, down_grad, qkv_grad, out_grad = grads
    results = (layer_out, tokens_grad)
    results += adam_step(*qkv, qkv_grad, D ** (-0.5))
    results += adam_step(*out, out_grad, (D // 32) ** (-0.5))
    results += adam_step(*up, up_grad, D ** (-0.5))
    results += adam_step(*down, down_grad, FF ** (-0.5))
    results += adam_step(*norm, norm_total[:4, :D], 0.2)
    return results


def solution(mesh):
    rows, both, flat = P(("dp", "tensor"), None), P("tensor", "dp"), P(("dp", "tensor"))
    state = (both,) * 8 + (flat,) * 8 + (P(),) * 4
    return jax.shard_map(
        on_device,
        mesh=mesh,
        in_specs=(rows, rows, P("dp"), P("dp"), P()) + state,
        out_specs=(rows, rows) + state,
        check_vma=False,
    )
```

```python
import functools

import jax
import jax.numpy as jnp
import numpy as np
from jax import lax
from jax.experimental import pallas as pl
from jax.experimental.pallas import tpu as pltpu
from jax.sharding import PartitionSpec as P

D = 480
HEAD = 24
FF = 1920
MAXLEN = 512
NDP, NTEN = 8, 4
WIDE = 512
HEADS_DEV = 5
LANES = 128
TILES = 47
JOINED = 1536
UP0, OUT0, DOWN0, QKV0 = 0, 15, 19, 35
CHUNK = 384
QB = 512
SPARE = 120

norm_eps = 1e-05
beta_one = 0.5
beta_two = 0.5
adam_eps = 1e-08
decay_rate = 0.01
average_keep = 0.75
hidden_score = -1e38
MESH = pl.DeviceIdType.MESH
f32, bf16 = jnp.float32, jnp.bfloat16


def mm(a, b):
    return lax.dot_general(a, b, (((1,), (0,)), ((), ())), preferred_element_type=f32)


def mm_nt(a, b):
    return lax.dot_general(a, b, (((1,), (1,)), ((), ())), preferred_element_type=f32)


def constants():
    natural = np.arange(D)
    squeeze = np.zeros((WIDE, WIDE), np.float32)
    squeeze[natural, 16 * (natural // 15) + natural % 15] = 1.0
    position = np.arange(MAXLEN, dtype=np.float32)
    exponent = np.arange(HEAD // 2, dtype=np.float32) * np.float32(2.0 / HEAD)
    inverse = np.float32(10000.0) ** (-exponent)
    angle = (position[:, None] * inverse[None, :]).astype(np.float32).astype(np.float64)
    lane = np.arange(120)
    place = lane % HEAD
    cosine = np.zeros((MAXLEN, LANES), np.float32)
    signed = np.zeros((MAXLEN, LANES), np.float32)
    cosine[:, :120] = np.cos(angle)[:, place % 12]
    signed[:, :120] = np.sin(angle)[:, place % 12] * np.where(place < 12, -1.0, 1.0)
    low = lambda v: jnp.asarray(v.astype(jnp.bfloat16))
    return (low(squeeze), jnp.asarray(cosine), jnp.asarray(signed))


UP, DOWN, EARLY, VALUES, OUT = (0, 1, 2), (3, 4, 5), (6, 7, 8), (9, 10), (11, 12)
WAY_A, WAY_B, WAY_C = (0, 1, 3, 2, 4), (0, 1, 2, 3, 4), (2, 3, 0, 1, 4)
GATHER_ROUTES = (
    (0, 8, WAY_A), (8, 8, WAY_B), (16, 3, WAY_C),
    (19, 6, WAY_A), (25, 7, WAY_B), (32, 3, WAY_C),
    (35, 3, WAY_A), (38, 3, WAY_B), (41, 2, WAY_C),
    (43, 2, WAY_A), (45, 2, WAY_B),
)
SCATTER_ROUTES = (
    (0, 6, WAY_A), (6, 6, WAY_B), (12, 3, WAY_C),
    (19, 6, WAY_A), (25, 7, WAY_B), (32, 3, WAY_C),
    (35, 3, WAY_A), (38, 3, WAY_B), (41, 2, WAY_C),
    (43, 2, WAY_A), (45, 2, WAY_B),
    (15, 2, WAY_A), (17, 2, WAY_B),
)
GATHER_AT = ((1, DOWN, 1), (3, UP, 3), (5, DOWN, 2), (10, UP, 4), (11, DOWN, 3), (18, DOWN, 4))
SCATTER_AT = ((2, OUT, 1), (5, UP, 2), (11, DOWN, 2), (13, OUT, 2), (14, UP, 3), (16, DOWN, 3), (17, OUT, 3), (18, UP, 4))


class Links:
    @staticmethod
    def scratch():
        n, tiles = len(SCATTER_ROUTES), (TILES, 16, LANES)
        bufs = [
            pltpu.VMEM((2,) * (4 - stage) + (count, 16, LANES), bf16)
            for begin, count, order in SCATTER_ROUTES
            for stage in range(5)
        ]
        return bufs + [
            pltpu.VMEM((2,) * 5 + tiles, bf16),
            pltpu.VMEM((2,) * 5 + tiles, bf16),
            pltpu.VMEM((3, 8, WIDE), f32),
            pltpu.VMEM((3, 4, 8, WIDE), f32),
            pltpu.SemaphoreType.DMA,
            pltpu.SemaphoreType.DMA((n, 5)),
            pltpu.SemaphoreType.DMA((n, 5)),
            pltpu.SemaphoreType.DMA((n, 5)),
            pltpu.SemaphoreType.DMA((n, 5)),
            pltpu.SemaphoreType.DMA((3, 3)),
            pltpu.SemaphoreType.DMA((3, 3)),
        ]

    def __init__(self, shard, total, norm_total, *scratch):
        n = len(SCATTER_ROUTES)
        self.shard, self.total, self.norm_total = shard, total, norm_total
        self.bufs = [scratch[5 * r : 5 * r + 5] for r in range(n)]
        (
            self.whole, self.parts, self.norm_now, self.norm_in, self.own_sem,
            self.g_send, self.g_recv, self.s_send, self.s_recv, self.n_send, self.n_recv,
        ) = scratch[5 * n :]
        dp, tensor = lax.axis_index("dp"), lax.axis_index("tensor")
        self.coords = (dp // 4, (dp // 2) % 2, dp % 2, tensor // 2, tensor % 2)

    def partner(self, dim):
        c = list(self.coords)
        c[dim] = 1 - c[dim]
        return (c[0] * 4 + c[1] * 2 + c[2], c[3] * 2 + c[4])

    def peers(self, group):
        z0, z1, x, y, core = self.coords
        found = []
        if group == 0:
            mine = z0 * 2 + z1
            for step in range(1, 4):
                z = (mine + step) % 4
                found.append(((z * 2 + x, y * 2 + core), z))
        elif group == 1:
            mine = x * 2 + y
            for dx, dy in ((0, 1), (1, 0), (1, 1)):
                px, py = (x + dx) % 2, (y + dy) % 2
                found.append((((z0 * 2 + z1) * 2 + px, py * 2 + core), px * 2 + py))
        else:
            mine = core
            found.append((((z0 * 2 + z1) * 2 + x, y * 2 + 1 - core), 1 - core))
        return found, mine

    def greet(self):
        barrier = pltpu.get_barrier_semaphore()
        others = [device for group in range(3) for device, slot in self.peers(group)[0]]
        for device in others:
            pl.semaphore_signal(barrier, inc=1, device_id=device, device_id_type=MESH)
        pl.semaphore_wait(barrier, len(others))

    def keep_own(self):
        copy = pltpu.make_async_copy(self.shard, self.whole.at[self.coords], self.own_sem)
        copy.start()
        copy.wait()

    def gather_copy(self, r, stage):
        begin, count, order = GATHER_ROUTES[r]
        done, dim = order[:stage], order[stage]
        where = tuple(slice(None) if d in done else self.coords[d] for d in range(5)) + (pl.ds(begin, count),)
        return pltpu.make_async_remote_copy(
            src_ref=self.whole.at[where],
            dst_ref=self.whole.at[where],
            send_sem=self.g_send.at[r, stage],
            recv_sem=self.g_recv.at[r, stage],
            device_id=self.partner(dim),
            device_id_type=MESH,
        )

    def gather_step(self, group, stage):
        for r in group:
            if stage > 0:
                self.gather_copy(r, stage - 1).wait_recv()
            if stage < 5:
                self.gather_copy(r, stage).start()

    def sums(self, r, stage, coordinate):
        begin, count, order = SCATTER_ROUTES[r]
        order = order[::-1]
        left = [d for d in range(5) if d not in order[:stage]]
        where = tuple(coordinate if d == order[stage] else slice(None) for d in left)
        if stage == 0:
            return self.parts.at[where + (pl.ds(begin, count),)]
        return self.bufs[r][stage - 1].at[where]

    def scatter_copy(self, r, stage):
        dim = SCATTER_ROUTES[r][2][4 - stage]
        return pltpu.make_async_remote_copy(
            src_ref=self.sums(r, stage, 1 - self.coords[dim]),
            dst_ref=self.bufs[r][stage],
            send_sem=self.s_send.at[r, stage],
            recv_sem=self.s_recv.at[r, stage],
            device_id=self.partner(dim),
            device_id_type=MESH,
        )

    def scatter_step(self, group, stage):
        for r in group:
            begin, count, order = SCATTER_ROUTES[r]
            if stage > 0:
                self.scatter_copy(r, stage - 1).wait_recv()
                buf = self.bufs[r][stage - 1]
                mine = self.sums(r, stage - 1, self.coords[order[5 - stage]])[...]
                if stage < 5:
                    buf[...] = buf[...] + mine
                else:
                    self.total[begin : begin + count] = buf[...].astype(f32) + mine.astype(f32)
            if stage < 5:
                self.scatter_copy(r, stage).start()

    def norm_copies(self, group):
        found, mine = self.peers(group)
        return [
            pltpu.make_async_remote_copy(
                src_ref=self.norm_now.at[group],
                dst_ref=self.norm_in.at[group, mine],
                send_sem=self.n_send.at[group, k],
                recv_sem=self.n_recv.at[group, k],
                device_id=device,
                device_id_type=MESH,
            )
            for k, (device, slot) in enumerate(found)
        ]

    def norm_start(self, values, group=0):
        self.norm_now[group] = values
        self.norm_in[group, self.peers(group)[1]] = values
        for copy in self.norm_copies(group):
            copy.start()

    def norm_step(self, group):
        for copy in self.norm_copies(group):
            copy.wait_recv()
        now = self.norm_in[group, 0]
        for slot in range(1, 2 if group == 2 else 4):
            now = now + self.norm_in[group, slot]
        if group < 2:
            self.norm_start(now, group + 1)
        else:
            self.norm_total[...] = now

    def finish(self):
        for stage in range(5):
            for r in range(len(GATHER_ROUTES)):
                self.gather_copy(r, stage).wait_send()
            for r in range(len(SCATTER_ROUTES)):
                self.scatter_copy(r, stage).wait_send()
        for group in range(3):
            for copy in self.norm_copies(group):
                copy.wait_send()


def gelu_parts(u):
    half = 0.5 * (1.0 + lax.erf(u * 0.7071067811865476))
    return u * half, half + u * jnp.exp(-0.5 * u * u) * 0.3989422804014327


def layer_kernel(remote, *refs):
    lengths, clusters, weights_of, source, tok, cot, norm, *tables = refs[:10]
    layer_out, tokens_grad, G_out, norm_out = refs[10:14]
    (
        up_s, down_s, qkv_s, dj_s, out_s, q_s, k_s, v_s, kT_s, vT_s, P_s, OT_s, att_s, dA_s, dqT_s, dk_s, dv_s,
        act1_s, act2_s, act_pad, plain1, plain2, res_s, y_s, dn_s, dres_s, dlow_s, eye_s, x_s, centre_s, ds_s, act_pad1, norm_s, rows_s, read_sem,
        widen, squeeze, cosine, signed,
    ) = refs[14:53]
    if remote:
        links = Links(source, G_out, norm_out, *refs[53:])
        W, G = links.whole, links.parts
        links.greet()
        links.keep_own()
        links.gather_step(EARLY, 0)
        links.gather_step(VALUES, 0)
    else:
        links, W, G = None, source, G_out
    me = lax.axis_index("tensor")
    length = lengths[me]
    scale_row = weights_of[clusters[me]]
    scale = HEAD ** -0.5

    lane = lax.broadcasted_iota(jnp.int32, (1, WIDE), 1)
    real = jnp.where(lane < D, 1.0, 0.0)
    norm_s[...] = jnp.zeros_like(norm_s)
    norm_s[:4, :D] = norm[...]
    gains = norm_s[...]

    def norm_rows(values, gain, shift):
        middle = jnp.sum(values, axis=-1, keepdims=True) * (1.0 / D)
        centered = (values - middle) * real
        spread_ = jnp.sum(centered * centered, axis=-1, keepdims=True) * (1.0 / D)
        inverse = lax.rsqrt(spread_ + norm_eps)
        plain = centered * inverse
        return plain * gain + shift, plain, inverse

    def norm_back(dz, plain, inverse, gain):
        dg = jnp.sum(dz * plain, axis=0, keepdims=True)
        db = jnp.sum(dz, axis=0, keepdims=True)
        scaled = dz * gain
        one = jnp.sum(scaled, axis=-1, keepdims=True) * (1.0 / D)
        two = jnp.sum(scaled * plain, axis=-1, keepdims=True) * (1.0 / D)
        return inverse * (scaled - one - plain * two) * real, dg, db

    places = (rows_s.at[0], rows_s.at[1], squeeze, cosine, signed)
    reads = [pltpu.make_async_copy(ref, to, read_sem.at[k]) for k, (ref, to) in enumerate(zip((tok, cot, *tables), places))]
    for read in reads:
        read.start()
    x_s[...] = jnp.zeros_like(x_s)
    dres_s[...] = jnp.zeros_like(dres_s)
    for read in reads:
        read.wait()
    x_s[:D, :] = rows_s[0].astype(f32)
    widen[...] = squeeze[...].astype(f32).T.astype(bf16)
    dres_s[:D, :] = rows_s[1].astype(f32)
    x_s[...] = x_s[...].T
    normed, plain, inverse1 = norm_rows(x_s[...], gains[0:1], gains[1:2])
    plain1[...] = plain
    act1_s[...] = normed.astype(bf16)
    if remote:
        links.gather_step(EARLY, 1)
        links.gather_step(VALUES, 1)
    row = lax.broadcasted_iota(jnp.int32, (MAXLEN, 1), 0)
    row_scale = jnp.where(row < length, scale_row, 0.0)
    dres_s[...] = dres_s[...].T * row_scale
    dlow_s[...] = dres_s[...].astype(bf16)
    act_pad1[...] = mm_nt(widen[...], act1_s[...]).astype(bf16)
    if remote:
        links.gather_step(EARLY, 2)
        links.gather_step(VALUES, 2)
        links.gather_step(UP, 0)
        links.gather_step(EARLY, 3)
        links.gather_step(VALUES, 3)
        links.gather_step(EARLY, 4)
        links.gather_step(VALUES, 4)
        links.gather_step(UP, 1)
        links.gather_step(EARLY, 5)
        links.gather_step(UP, 2)
        links.gather_step(DOWN, 0)

    def joined_third(c):
        pieces = []
        for t in range(NTEN):
            mine = (slice(None),) * 3 + (t // 2, t % 2)
            pieces.append(W[mine + (slice(QKV0 + 4 * c, QKV0 + 4 * c + 4),)].reshape(WIDE, LANES))
        third = slice(c * WIDE, (c + 1) * WIDE)
        qkv_s[:, third] = mm(squeeze[...], jnp.concatenate(pieces, 1)).astype(bf16)
        return mm(act1_s[...], qkv_s[:, third])

    cosv, signv = cosine[...], signed[...]
    lane_id = lax.broadcasted_iota(jnp.int32, (1, LANES), 1)
    ahead = functools.reduce(jnp.logical_or, [(lane_id >= j * HEAD) & (lane_id < j * HEAD + HEAD // 2) for j in range(HEADS_DEV)])

    def partners(u):
        return jnp.where(ahead, pltpu.roll(u, LANES - HEAD // 2, 1), pltpu.roll(u, HEAD // 2, 1))

    key_id = lax.broadcasted_iota(jnp.int32, (MAXLEN, 1), 0)
    spare = jnp.where(lane_id == SPARE, 1.0, 0.0)
    key_bias = jnp.where(key_id < length, 0.0, hidden_score) * spare

    def strided(block):
        gap = jnp.zeros((8, MAXLEN), f32)
        return jnp.concatenate([x for j in range(HEADS_DEV) for x in (block[j * HEAD : (j + 1) * HEAD], gap)], 0)

    def dense(block):
        rows = [block[j * 32 : j * 32 + HEAD] for j in range(HEADS_DEV)]
        return jnp.concatenate(rows + [jnp.zeros((8, MAXLEN), f32)], 0)

    for number in range(2):
        joined = joined_third(number)
        for t in range(NTEN):
            u = joined[:, t * LANES : (t + 1) * LANES]
            r = u * cosv + partners(u) * signv
            if number == 0:
                q_s[t] = (r + spare).astype(bf16)
            else:
                k_s[t] = (r + key_bias).astype(bf16)
                kT_s[t] = strided(r.T).astype(bf16)
    if remote:
        links.gather_step(VALUES, 5)
    joined = joined_third(2)
    for t in range(NTEN):
        v = joined[:, t * LANES : (t + 1) * LANES]
        v_s[t] = v.astype(bf16)
        vT_s[t] = strided(v.T).astype(bf16)

    OT_s[...] = jnp.zeros_like(OT_s)
    fold = HEAD ** -0.5 * 1.4426950408889634

    def forward_head(h, carry):
        t = h // HEADS_DEV
        j = h - t * HEADS_DEV
        begin = j * HEAD
        kept = ((lane_id >= begin) & (lane_id < begin + HEAD)) | (lane_id == SPARE)
        keys = k_s[t] * jnp.where(kept, 1.0, 0.0).astype(bf16)
        rows = pl.ds(pl.multiple_of(j * 32, 32), 32)
        values = vT_s[t, rows, :]
        for b in range(MAXLEN // QB):
            cols = slice(b * QB, (b + 1) * QB)
            s = mm_nt(keys, q_s[t, cols, :])
            top = jnp.max(s, axis=0, keepdims=True)
            e = jnp.exp2(s * fold - top * fold)
            total = jnp.sum(e, axis=0, keepdims=True)
            p = (e * (1.0 / total)).astype(bf16)
            P_s[h, :, cols] = p
            OT_s[t, rows, cols] = mm(values, p)
        if remote:
            for when, group, number in GATHER_AT:
                pl.when(h == when)(functools.partial(links.gather_step, group, number))
        return carry

    lax.fori_loop(0, NTEN * HEADS_DEV, forward_head, 0)

    if remote:
        links.gather_step(UP, 5)
    res = x_s[...]
    for t in range(NTEN):
        mine = (slice(None),) * 3 + (t // 2, t % 2)
        pieces = [W[mine + (OUT0 + c,)].reshape(LANES, LANES) for c in range(4)]
        out_s[t] = mm(squeeze[:LANES, :LANES], jnp.concatenate(pieces, 1)).astype(bf16)
        att_s[t] = dense(OT_s[t]).T.astype(bf16)
        res = res + mm(att_s[t], out_s[t])
    res_s[...] = res
    normed, plain, inverse2 = norm_rows(res, gains[2:3], gains[3:4])
    plain2[...] = plain
    act2_s[...] = normed.astype(bf16)
    act_pad[...] = mm_nt(widen[...], act2_s[...]).astype(bf16)

    for c in range(8):
        pieces = [W[:, :, :, :, :, UP0 + n].reshape(WIDE, LANES) for n in range(2 * c, min(2 * c + 2, 15))]
        up_s[:, 2 * c * LANES : (2 * c + len(pieces)) * LANES] = mm(squeeze[...], jnp.concatenate(pieces, 1)).astype(bf16)

    if remote:
        links.gather_step(DOWN, 5)

    def down_rows(k, carry):
        mine = (k // 4, (k // 2) % 2, k % 2)
        pieces = [W[mine + (slice(None),) * 2 + (slice(DOWN0 + 4 * c, DOWN0 + 4 * c + 4),)].reshape(256, LANES) for c in range(4)]
        part = mm(squeeze[:240, :256], jnp.concatenate(pieces, 1)).astype(bf16)
        down_s[pl.ds(pl.multiple_of(k * 240, 16), 240), :] = part
        return carry

    lax.fori_loop(0, NDP, down_rows, 0)

    y_s[...] = res_s[...]
    dn_s[...] = jnp.zeros_like(dn_s)
    eye_row = lax.broadcasted_iota(jnp.int32, (CHUNK, CHUNK), 0)
    eye_col = lax.broadcasted_iota(jnp.int32, (CHUNK, CHUNK), 1)
    eye = jnp.where(eye_row == eye_col, 1.0, 0.0).astype(bf16)
    eye_s[...] = eye

    def hidden_chunk(c, carry):
        cols = pl.ds(pl.multiple_of(c * CHUNK, LANES), CHUNK)
        u = mm(act2_s[...], up_s[:, cols])
        value, slope = gelu_parts(u)
        a = value.astype(bf16)
        y_s[...] += mm(a, down_s[cols, :])
        d_active = mm_nt(dlow_s[...], down_s[cols, :])
        d_upper = (d_active * slope).astype(bf16)
        dn_s[...] += mm_nt(d_upper, up_s[:, cols])
        g_up = mm(act_pad[...], d_upper).astype(bf16)
        for part in range(3):
            G[:, :, :, :, :, UP0 + 3 * c + part] = g_up[:, part * LANES : (part + 1) * LANES].reshape(2, 2, 2, 2, 2, 16, LANES)
        aT = mm_nt(eye_s[...], a).astype(bf16)
        down_s[cols, :] = mm(aT, dlow_s[...]).astype(bf16)
        return carry

    lax.fori_loop(0, FF // CHUNK, hidden_chunk, 0)
    if remote:
        links.scatter_step(UP, 0)
    y_s[...] = y_s[...].T
    layer_out[...] = y_s[:D, :]

    def down_groups(k, carry):
        part = mm(widen[:256, :240], down_s[pl.ds(pl.multiple_of(k * 240, 16), 240), :]).astype(bf16)
        mine = (k // 4, (k // 2) % 2, k % 2)
        for c in range(4):
            where = mine + (slice(None),) * 2 + (slice(DOWN0 + 4 * c, DOWN0 + 4 * c + 4),)
            G[where] = part[:, c * LANES : (c + 1) * LANES].reshape(2, 2, 4, 16, LANES)
        return carry

    lax.fori_loop(0, NDP, down_groups, 0)
    if remote:
        links.scatter_step(DOWN, 0)

    d_from, dg2, db2 = norm_back(dn_s[...], plain2[...], inverse2, gains[2:3])
    d_res = dres_s[...] + d_from
    dres_s[...] = d_res
    dlow_s[...] = d_res.astype(bf16)

    if remote:
        links.scatter_step(UP, 1)
    for t in range(NTEN):
        dA_s[t] = mm_nt(dlow_s[...], out_s[t]).astype(bf16)
        dAT = mm_nt(out_s[t], dlow_s[...]).astype(bf16).astype(f32)
        product = OT_s[t] * strided(dAT)
        for j in range(HEADS_DEV):
            centre_s[t, j : j + 1, :] = jnp.sum(product[j * 32 : j * 32 + HEAD], axis=0, keepdims=True)
        attT = mm_nt(widen[:LANES, :LANES], att_s[t]).astype(bf16)
        part = mm(attT, dlow_s[...]).astype(bf16)
        mine = (slice(None),) * 3 + (t // 2, t % 2)
        for c in range(4):
            G[mine + (OUT0 + c,)] = part[:, c * LANES : (c + 1) * LANES].reshape(2, 2, 2, 16, LANES)
    if remote:
        links.scatter_step(OUT, 0)
        links.scatter_step(DOWN, 1)

    dk_s[...] = jnp.zeros_like(dk_s)
    dv_s[...] = jnp.zeros_like(dv_s)

    def backward_head(h, carry):
        t = h // HEADS_DEV
        j = h - t * HEADS_DEV
        begin = j * HEAD
        lanes = jnp.where((lane_id >= begin) & (lane_id < begin + HEAD), 1.0, 0.0).astype(bf16)
        rows = pl.ds(pl.multiple_of(j * 32, 32), 32)
        values = v_s[t]
        keysT = kT_s[t, rows, :]
        dA = dA_s[t] * lanes
        for b in range(MAXLEN // QB):
            cols = slice(b * QB, (b + 1) * QB)
            dP = mm_nt(values, dA[cols])
            ds = (P_s[h, :, cols].astype(f32) * (dP - centre_s[t, pl.ds(j, 1), cols])).astype(bf16)
            ds_s[:, cols] = ds
            dqT_s[t, rows, cols] = mm(keysT, ds)
        dv_s[t] += mm(P_s[h], dA)
        dk_s[t] += mm(ds_s[...], q_s[t] * lanes)
        if remote:
            for when, group, number in SCATTER_AT:
                pl.when(h == when)(functools.partial(links.scatter_step, group, number))
        return carry

    lax.fori_loop(0, NTEN * HEADS_DEV, backward_head, 0)

    def scatter_third(c):
        part = mm(act_pad1[...], dj_s[:, c * WIDE : (c + 1) * WIDE]).astype(bf16)
        for t in range(NTEN):
            where = (slice(None),) * 3 + (t // 2, t % 2) + (slice(QKV0 + 4 * c, QKV0 + 4 * c + 4),)
            G[where] = part[:, t * LANES : (t + 1) * LANES].reshape(2, 2, 2, 4, 16, LANES)

    for t in range(NTEN):
        dj_s[:, 2 * WIDE + t * LANES : 2 * WIDE + (t + 1) * LANES] = dv_s[t].astype(bf16)
    scatter_third(2)
    if remote:
        links.scatter_step(VALUES, 0)
    for number in (1, 0):
        for t in range(NTEN):
            g = (dense(dqT_s[t]).T if number == 0 else dk_s[t]) * scale
            r = g * cosv - partners(g) * signv
            dj_s[:, number * WIDE + t * LANES : number * WIDE + (t + 1) * LANES] = r.astype(bf16)
        scatter_third(number)
    if remote:
        links.scatter_step(EARLY, 0)
        links.scatter_step(VALUES, 1)
        links.scatter_step(UP, 5)
        links.scatter_step(DOWN, 4)
        links.scatter_step(OUT, 4)
    dz = mm_nt(dj_s[...], qkv_s[...])
    d_from, dg1, db1 = norm_back(dz, plain1[...], inverse1, gains[0:1])
    norm_parts = jnp.concatenate([dg1, db1, dg2, db2, jnp.zeros((4, WIDE), f32)], 0)
    if remote:
        links.norm_start(norm_parts)
        links.scatter_step(EARLY, 1)
    else:
        norm_out[...] = norm_parts
    x_s[...] = (dres_s[...] + d_from).T
    tokens_grad[...] = x_s[:D, :]
    if remote:
        links.norm_step(0)
        links.scatter_step(DOWN, 5)
        links.scatter_step(OUT, 5)
        links.scatter_step(VALUES, 2)
        links.scatter_step(EARLY, 2)
        links.norm_step(1)
        links.scatter_step(VALUES, 3)
        links.scatter_step(EARLY, 3)
        links.norm_step(2)
        links.scatter_step(VALUES, 4)
        links.scatter_step(EARLY, 4)
        links.scatter_step(VALUES, 5)
        links.scatter_step(EARLY, 5)
        links.finish()


def run_layer(lengths, clusters, cluster_weight, source, tokens, cotangent, norm_master, remote):
    rows = MAXLEN
    smem = pl.BlockSpec(memory_space=pltpu.SMEM)
    vmem = pl.BlockSpec(memory_space=pltpu.VMEM)
    hbm = pl.BlockSpec(memory_space=pl.ANY)
    head_set = (NTEN, MAXLEN, LANES)
    turned = (NTEN, HEADS_DEV * 32, MAXLEN)
    wide = (rows, WIDE)
    scratch = [
        pltpu.VMEM((WIDE, FF), bf16),
        pltpu.VMEM((FF, WIDE), bf16),
        pltpu.VMEM((WIDE, JOINED), bf16),
        pltpu.VMEM((WIDE, JOINED), bf16),
        pltpu.VMEM((NTEN, LANES, WIDE), bf16),
        pltpu.VMEM(head_set, bf16),
        pltpu.VMEM(head_set, bf16),
        pltpu.VMEM(head_set, bf16),
        pltpu.VMEM(turned, bf16),
        pltpu.VMEM(turned, bf16),
        pltpu.VMEM((NTEN * HEADS_DEV, MAXLEN, MAXLEN), bf16),
        pltpu.VMEM(turned, f32),
        pltpu.VMEM(head_set, bf16),
        pltpu.VMEM(head_set, bf16),
        pltpu.VMEM(turned, f32),
        pltpu.VMEM(head_set, f32),
        pltpu.VMEM(head_set, f32),
        pltpu.VMEM(wide, bf16),
        pltpu.VMEM(wide, bf16),
        pltpu.VMEM(wide, bf16),
        pltpu.VMEM(wide, f32),
        pltpu.VMEM(wide, f32),
        pltpu.VMEM(wide, f32),
        pltpu.VMEM(wide, f32),
        pltpu.VMEM(wide, f32),
        pltpu.VMEM(wide, f32),
        pltpu.VMEM(wide, bf16),
        pltpu.VMEM((CHUNK, CHUNK), bf16),
        pltpu.VMEM(wide, f32),
        pltpu.VMEM((NTEN, 8, MAXLEN), f32),
        pltpu.VMEM((MAXLEN, MAXLEN), bf16),
        pltpu.VMEM(wide, bf16),
        pltpu.VMEM((8, WIDE), f32),
        pltpu.VMEM((2, D, MAXLEN), bf16),
        pltpu.SemaphoreType.DMA((5,)),
        pltpu.VMEM((WIDE, WIDE), bf16),
        pltpu.VMEM((WIDE, WIDE), bf16),
        pltpu.VMEM((MAXLEN, LANES), f32),
        pltpu.VMEM((MAXLEN, LANES), f32),
    ]
    tiles = (TILES, 16, LANES)
    params = dict(vmem_limit_bytes=66_900_000)
    if remote:
        result = jax.ShapeDtypeStruct(tiles, f32)
        scratch += Links.scratch()
        params.update(collective_id=0, has_side_effects=True)
    else:
        result = jax.ShapeDtypeStruct((2,) * 5 + tiles, bf16)
        source = source.reshape((2,) * 5 + tiles)
    turned_out, turned_grad, grads, norm_grad = pl.pallas_call(
        functools.partial(layer_kernel, remote),
        out_shape=(
            jax.ShapeDtypeStruct((D, rows), f32),
            jax.ShapeDtypeStruct((D, rows), f32),
            result,
            jax.ShapeDtypeStruct((8, WIDE), f32),
        ),
        in_specs=[smem] * 3 + [vmem, hbm, hbm, vmem] + [hbm] * 3,
        out_specs=[vmem] * 4,
        scratch_shapes=scratch,
        compiler_params=pltpu.CompilerParams(**params),
        name="layer",
    )(lengths, clusters, cluster_weight, source, tokens.T, cotangent.T, norm_master, *constants())
    if not remote:
        grads = grads.reshape(NDP, NTEN, *tiles)
    return turned_out.T, turned_grad.T, grads, norm_grad


def shard_tiles(up, down, qkv, out):
    up = jnp.pad(up.reshape(15, 15, LANES), ((0, 1), (0, 0), (0, 0))).transpose(1, 0, 2)
    down = jnp.pad(down.reshape(4, 15, D), ((0, 0), (0, 1), (0, WIDE - D)))
    down = down.reshape(4, 16, 4, LANES).transpose(2, 0, 1, 3).reshape(16, 16, LANES)
    qkv = jnp.pad(qkv.reshape(4, 15, 3, 120), ((0, 0), (0, 1), (0, 0), (0, LANES - 120)))
    qkv = qkv.transpose(2, 0, 1, 3).reshape(12, 16, LANES)
    out = jnp.pad(out.reshape(15, D), ((0, 1), (0, WIDE - D)))
    out = out.reshape(16, 4, LANES).transpose(1, 0, 2)
    return jnp.concatenate([up, out, down, qkv], 0)


def tiles_shard(tiles):
    up = tiles[UP0:OUT0, :15].transpose(1, 0, 2).reshape(-1)
    down = tiles[DOWN0:QKV0].reshape(4, 4, 16, LANES).transpose(1, 2, 0, 3)[:, :15].reshape(60, WIDE)[:, :D].reshape(-1)
    qkv = tiles[QKV0:].reshape(3, 4, 16, LANES).transpose(1, 2, 0, 3)[:, :15, :, :120].reshape(1, -1)
    out = tiles[OUT0:DOWN0].transpose(1, 0, 2)[:15].reshape(15, WIDE)[:, :D].reshape(1, -1)
    return up, down, qkv, out


def adam_step(master, moment, square, average, grad, rate):
    moment_new = beta_one * moment + (1.0 - beta_one) * grad
    square_new = beta_two * square + (1.0 - beta_two) * grad * grad
    update = moment_new / (jnp.sqrt(square_new) + adam_eps) + decay_rate * master
    fresh = master - rate * update
    average_new = average_keep * average + (1.0 - average_keep) * fresh
    return (fresh, moment_new, square_new, average_new)


def to_groups(up, down, qkv, out):
    up, down = up.reshape(NDP, NTEN, -1), down.reshape(NDP, NTEN, -1)
    qkv = qkv.reshape(NTEN, NDP, -1).transpose(1, 0, 2)
    out = out.reshape(NTEN, NDP, -1).transpose(1, 0, 2)
    return jax.vmap(jax.vmap(shard_tiles))(up, down, qkv, out)


def from_groups(tiles):
    up, down, qkv, out = jax.vmap(jax.vmap(tiles_shard))(tiles.astype(f32))
    qkv = qkv.reshape(NDP, NTEN, -1).transpose(1, 0, 2).reshape(NTEN, -1)
    out = out.reshape(NDP, NTEN, -1).transpose(1, 0, 2).reshape(NTEN, -1)
    return up.reshape(-1), down.reshape(-1), qkv, out


def on_device(tokens, cotangent, lengths, clusters, cluster_weight, *state):
    qkv, out, up, down, norm = (state[4 * k : 4 * k + 4] for k in range(5))
    ends = ("dp", "tensor")
    low = tuple(w[0].astype(bf16) for w in (up, down, qkv, out))
    grid = (lax.axis_size("dp"), lax.axis_size("tensor")) == (NDP, NTEN)
    if grid:
        source = shard_tiles(*low)
    else:
        whole = [lax.all_gather(w, ends, axis=0, tiled=True) for w in low[:2]]
        for w in low[2:]:
            block = lax.all_gather(w, "dp", axis=1, tiled=True)
            whole.append(lax.all_gather(block, "tensor", axis=0, tiled=True))
        source = to_groups(*whole)
    layer_out, tokens_grad, total, norm_total = run_layer(
        lengths, clusters, cluster_weight, source, tokens, cotangent, norm[0], grid
    )
    if grid:
        grads = tiles_shard(total)
    else:
        whole = from_groups(total)
        grads = [lax.psum_scatter(g, ends, scatter_dimension=0, tiled=True) for g in whole[:2]]
        for g in whole[2:]:
            block = lax.psum_scatter(g, "tensor", scatter_dimension=0, tiled=True)
            grads.append(lax.psum_scatter(block, "dp", scatter_dimension=1, tiled=True))
        norm_total = lax.psum(norm_total, ends)
    up_grad, down_grad, qkv_grad, out_grad = grads
    results = (layer_out, tokens_grad)
    results += adam_step(*qkv, qkv_grad, D ** (-0.5))
    results += adam_step(*out, out_grad, (D // 32) ** (-0.5))
    results += adam_step(*up, up_grad, D ** (-0.5))
    results += adam_step(*down, down_grad, FF ** (-0.5))
    results += adam_step(*norm, norm_total[:4, :D], 0.2)
    return results


def solution(mesh):
    rows, both, flat = P(("dp", "tensor"), None), P("tensor", "dp"), P(("dp", "tensor"))
    state = (both,) * 8 + (flat,) * 8 + (P(),) * 4
    return jax.shard_map(
        on_device,
        mesh=mesh,
        in_specs=(rows, rows, P("dp"), P("dp"), P()) + state,
        out_specs=(rows, rows) + state,
        check_vma=False,
    )
```
